512 devices in a mesh: freq: 32 (over z, core), rows: 16 (over y, x).
Axes of the slice: x: 4, y: 4, z: 16, core: 2. Of those that a mesh axis runs over, the one named last changes fastest.
Arguments:
- wavefield: float32 [2, 32, 1024, 2048], P(None, 'freq', 'rows'), may hold values from -28 to 28
- block_inverse: bfloat16 [2, 32, 16, 128, 128], P(None, 'freq'), may hold values from -0.19921875 to 0.19921875
- coefficient: bfloat16 [1024, 2048], P('rows'), may hold values from 0.049804688 to 0.29882812
- correction_factor: float32 [2, 32], P(None, 'freq'), may hold values from -4 to 4
- frequencies: float32 [32], P('freq'), may hold values from 1.5 to 4.5
- slowness: float32 [2], replicated, may hold values from 0.7 to 1
Outputs:
- depth_image: float32 [2, 1024, 2048], P(None, 'rows', 'freq')
- final_field: float32 [2, 32, 1024, 2048], P(None, 'freq', 'rows')
The draws below stay inside these ranges and needn't reach their ends.
All inputs are finite; a program needn't handle non-finite values.
Results may differ from the reference program's by a relative error of at most 0.023.
Values may be sent and summed in bfloat16 or wider, within the bound.
A program may use at most 64 MiB of HBM per device.

```python
import math
import jax
import jax.numpy as jnp
from jax import lax

NX = 2048
NY = 1024
BLOCK = 128
DEPTHS = 2
NW = 32


def draw_wavefield(key, part):
    noise_key = jax.random.fold_in(key, 11)
    column_key = jax.random.fold_in(key, 12)
    common_key = jax.random.fold_in(key, 13)
    region_key = jax.random.fold_in(key, 14)
    position = jnp.arange(NY, dtype=jnp.float32) / max(NY - 1, 1)
    column_scale = 10.0 ** jax.random.uniform(column_key, (NX,), jnp.float32)
    region_pick = jax.random.randint(region_key, (4, 16), 0, 10)
    region_weight = jnp.where(region_pick < 3, 0.95, 0.15).astype(jnp.float32)
    row_quarter = jnp.arange(NY, dtype=jnp.int32) * 4 // NY
    column_block = jnp.arange(NX, dtype=jnp.int32) * 16 // NX
    shared_weight = region_weight[row_quarter][:, column_block]
    own_weight = jnp.sqrt(1.0 - shared_weight * shared_weight)
    base_noise = jnp.clip(jax.random.normal(noise_key, (2, NW, NY, NX), jnp.float32), -6.0, 6.0)
    common_noise = jnp.clip(jax.random.normal(common_key, (2, 1, NY, NX), jnp.float32), -6.0, 6.0)
    base_noise = jnp.clip(own_weight * base_noise + shared_weight * common_noise, -6.0, 6.0)
    row_scale = 10.0 ** position
    return base_noise * (row_scale[:, None] * column_scale[None, :]) / 21.5


def block_levels(rng, extent, pieces, low, largest):
    factor_of, own = 1.0, jax.random.fold_in(rng, 6)
    for dim, blocks in pieces:
        steps = jnp.exp(jax.random.uniform(jax.random.fold_in(own, dim), (blocks,), jnp.float32, low / len(pieces), largest / len(pieces)))
        factor_of = factor_of * jnp.repeat(steps, extent[dim] // blocks).reshape([-1 if axis == dim else 1 for axis in range(len(extent))])
    return factor_of


def centred(key, dims, deviation, bound, cuts=(), kind=jnp.bfloat16):
    gain = block_levels(key, dims, cuts, -0.22, 0.18) if cuts else 1.0
    values = jax.random.normal(key, dims, jnp.float32) * deviation * gain
    return jnp.minimum(jnp.maximum(values, -bound), bound).astype(kind)


def setup_inputs(seed: int = 0) -> dict:
    splits = jax.random.split(jax.random.key(seed), 7)
    return {
        "wavefield": draw_wavefield(jax.random.fold_in(splits[6], 71), 0),
        "block_inverse": centred(splits[1], (2, NW, NX // BLOCK, BLOCK, BLOCK), 0.03, 0.19921875, ((1, 32),)),
        "coefficient": jnp.clip(jnp.exp(math.log(0.29882812) - 1.7917595 * jax.random.uniform(splits[2], (NY, NX), jnp.float32) ** block_levels(splits[2], (NY, NX), ((0, 16),), -0.2, 0.2)), 0.049804688, 0.29882812).astype(jnp.bfloat16),
        "correction_factor": centred(splits[3], (2, NW), 1.0, 4.0, ((1, 32),), jnp.float32),
        "frequencies": jnp.clip(1.5 + 3.0 * jax.random.uniform(splits[4], (NW,), jnp.float32) ** block_levels(splits[4], (NW,), ((0, 32),), -0.2, 0.2), 1.5, 4.5),
        "slowness": jnp.clip(jax.random.uniform(splits[5], (DEPTHS,), jnp.float32, 0.7, 1.0), 0.7, 1.0),
    }


def wavenumbers(length, offset, count):
    indices = offset + jnp.arange(count, dtype=jnp.int32)
    signed = jnp.where(2 * indices < length, indices, indices - length)
    return signed.astype(jnp.float32) * (2.0 * jnp.pi / length)

def to_bfloat(values):
    return lax.optimization_barrier(values.astype(jnp.bfloat16)).astype(jnp.float32)

def blockwise(left_rows, right_blocks):
    return jnp.einsum('ybi,bij->ybj', left_rows, right_blocks, precision=lax.Precision.HIGHEST)

def reference(wavefield, block_inverse, coefficient, correction_factor, frequencies, slowness):
    kappa_y = wavenumbers(NY, 0, NY)
    kappa_x = wavenumbers(NX, 0, NX)
    coef_full = coefficient.astype(jnp.float32)
    block_count = NX // BLOCK

    def one_frequency(image_sums, freq_index):
        field_pair = lax.dynamic_index_in_dim(wavefield, freq_index, 1, keepdims=False)
        block_pair = lax.dynamic_index_in_dim(block_inverse, freq_index, 1, keepdims=False).astype(jnp.float32)
        factor_pair = lax.dynamic_index_in_dim(correction_factor, freq_index, 1, keepdims=False)
        omega_value = lax.dynamic_index_in_dim(frequencies, freq_index, 0, keepdims=False)
        real_part = field_pair[0]
        imag_part = field_pair[1]
        for depth_step in range(DEPTHS):
            spectrum = jnp.fft.fft(real_part + 1j * imag_part, axis=1)
            spectrum = to_bfloat(spectrum.real) + 1j * to_bfloat(spectrum.imag)
            spectrum = jnp.fft.fft(spectrum, axis=0)
            vertical = (omega_value * slowness[depth_step]) ** 2 - kappa_y[:, None] ** 2 - kappa_x[None, :] ** 2
            root_value = jnp.sqrt(jnp.abs(vertical))
            upward = vertical >= 0.0
            prop_real = jnp.where(upward, jnp.cos(root_value), jnp.exp(-root_value))
            prop_imag = jnp.where(upward, jnp.sin(root_value), 0.0)
            spectrum = spectrum * (prop_real + 1j * prop_imag)
            returned = jnp.fft.ifft(spectrum, axis=0)
            returned = to_bfloat(returned.real) + 1j * to_bfloat(returned.imag)
            space_field = jnp.fft.ifft(returned, axis=1)
            space_real = space_field.real
            space_imag = space_field.imag
            padded_real = jnp.pad(space_real, ((1, 1), (0, 0)))
            padded_imag = jnp.pad(space_imag, ((1, 1), (0, 0)))
            curve_real = padded_real[2:] - 2.0 * space_real + padded_real[:-2]
            curve_imag = padded_imag[2:] - 2.0 * space_imag + padded_imag[:-2]
            corrected_real = space_real + coef_full * (factor_pair[0] * curve_real - factor_pair[1] * curve_imag)
            corrected_imag = space_imag + coef_full * (factor_pair[0] * curve_imag + factor_pair[1] * curve_real)
            rounded_real = to_bfloat(corrected_real).reshape(NY, block_count, BLOCK)
            rounded_imag = to_bfloat(corrected_imag).reshape(NY, block_count, BLOCK)
            new_real = corrected_real + (blockwise(rounded_real, block_pair[0]) - blockwise(rounded_imag, block_pair[1])).reshape(NY, NX)
            new_imag = corrected_imag + (blockwise(rounded_real, block_pair[1]) + blockwise(rounded_imag, block_pair[0])).reshape(NY, NX)
            image_sums = image_sums.at[depth_step].add(new_real)
            real_part = new_real
            imag_part = new_imag
        return (image_sums, jnp.stack([real_part, imag_part]))
    start_sums = jnp.zeros((DEPTHS, NY, NX), jnp.float32)
    image_sums, finals = lax.scan(one_frequency, start_sums, jnp.arange(NW, dtype=jnp.int32))
    energy = lax.optimization_barrier(jnp.mean(image_sums * image_sums, axis=(1, 2), keepdims=True))
    depth_image = image_sums / jnp.sqrt(energy + 1e-06)
    return (depth_image, jnp.moveaxis(finals, 0, 1))
```

```python
import math

import jax
import jax.numpy as jnp
import numpy as np
from jax import lax
from jax.experimental import pallas as pl
from jax.experimental.pallas import tpu as pltpu
from jax.sharding import PartitionSpec as P

MESH = pl.DeviceIdType.MESH
F32 = jnp.float32
BF16 = jnp.bfloat16
NX = 2048
NY = 1024
DEPTHS = 2
ROWS = 16
FREQ = 32
CHIPS = 16
EPS = 1e-06


def tables():
    b, k2 = np.arange(128)[:, None], np.arange(128)[None, :]
    fwd, inv = [], []
    for k1 in range(16):
        angle = -2.0 * np.pi * ((b * (k1 + 16 * k2)) % NX) / NX
        re, im = np.cos(angle), np.sin(angle)
        block = np.block([[re, im], [-im, re]])
        fwd.append(block)
        inv.append(block.T / NX)
    k2, b = np.arange(256)[:, None], np.arange(256)[None, :]
    yfwd, yinv = [], []
    for k1 in range(4):
        angle = -2.0 * np.pi * ((b * (k1 + 4 * k2)) % NY) / NY
        re, im = np.cos(angle), np.sin(angle)
        yfwd.append(np.concatenate([re, im], 0))
        yinv.append(np.concatenate([re.T, -im.T], 0) / NY)
    return [np.stack(t).astype(np.float32) for t in (fwd, inv, yfwd, yinv)]


def add(p, q):
    return p[0] + q[0], p[1] + q[1]


def sub(p, q):
    return p[0] - q[0], p[1] - q[1]


def fft4(x, sign):
    a, b = add(x[0], x[2]), sub(x[0], x[2])
    c, d = add(x[1], x[3]), sub(x[1], x[3])
    turned = (-sign * d[1], sign * d[0]) if sign > 0 else (d[1], -d[0])
    return [add(a, c), add(b, turned), sub(a, c), sub(b, turned)]


def twist(p, m, sign):
    re, im = p
    if m == 0:
        return p
    if m == 4:
        return (-im, re) if sign > 0 else (im, -re)
    if m == 2:
        h = math.sqrt(0.5)
        return ((re - im) * h, (re + im) * h) if sign > 0 else ((re + im) * h, (im - re) * h)
    c, s = math.cos(2 * math.pi * m / 16), sign * math.sin(2 * math.pi * m / 16)
    return re * c - im * s, re * s + im * c


def fft16(x, sign):
    inner = [fft4([x[4 * n1 + n2] for n1 in range(4)], sign) for n2 in range(4)]
    out = [None] * 16
    for k1 in range(4):
        got = fft4([twist(inner[n2][k1], n2 * k1, sign) for n2 in range(4)], sign)
        for k2 in range(4):
            out[k1 + 4 * k2] = got[k2]
    return out


def sin_cos(r):
    n = jnp.floor(r * (2.0 / math.pi) + 0.5)
    t = (r - n * 1.5703125) - n * (math.pi / 2 - 1.5703125)
    t2 = t * t
    sine = t + t * t2 * (-1 / 6 + t2 * (1 / 120 + t2 * (-1 / 5040 + t2 * (1 / 362880))))
    cosine = 1.0 + t2 * (-0.5 + t2 * (1 / 24 + t2 * (-1 / 720 + t2 * (1 / 40320))))
    m = n - 4.0 * jnp.floor(n * 0.25)
    odd = (m == 1.0) | (m == 3.0)
    s, c = jnp.where(odd, cosine, sine), jnp.where(odd, sine, cosine)
    return jnp.where(m >= 2.0, -s, s), jnp.where((m == 1.0) | (m == 2.0), -c, c)


def kernel(
    wf, bi, coef, cf, fr, sl, tx_h, txi_h, ty_h, tyi_h,
    img, fin,
    field, tx, txi, ty, tyi, wb, xb, sa, ra, yb, cc, uu, cb, gg, se, re_, sh, rh, gx, sp,
    ia_s, ia_r, ib_s, ib_r, qq, qp, en_s, en_r, et_s, et_r,
    in_sem, tab_sem, a_ss, a_rs, e_ss, e_rs, h_ss, h_rs, ia_sem, ib_ss, ib_rs, q_sem,
    d_ss, d_rs, t_ss, t_rs, out_sem,
):
    me = lax.axis_index("rows")
    fq = lax.axis_index("freq")
    my_y, my_x = me // 4, lax.rem(me, 4)
    chip, core = fq // 2, lax.rem(fq, 2)
    partner = chip * 2 + (1 - core)

    barrier = pltpu.get_barrier_semaphore()

    def greet_rows(o, _):
        pl.semaphore_signal(barrier, inc=1, device_id={"rows": lax.rem(me + o, ROWS)}, device_id_type=MESH)
        return 0

    def greet_freq(o, _):
        pl.semaphore_signal(barrier, inc=1, device_id={"freq": lax.rem(fq + o, FREQ)}, device_id_type=MESH)
        return 0

    lax.fori_loop(1, FREQ, greet_freq, 0)
    lax.fori_loop(1, ROWS, greet_rows, 0)

    loads = []
    for part in range(2):
        for a in range(16):
            loads.append(pltpu.make_async_copy(
                wf.at[part, 0, :, pl.ds(128 * a, 128)],
                field.at[a, :, pl.ds(128 * part, 128)], in_sem.at[part, a]))
    more = [pltpu.make_async_copy(s, d, tab_sem.at[i]) for i, (s, d) in enumerate((
        (tx_h, tx), (ty_h, ty), (tyi_h, tyi), (txi_h, txi),
        (bi.at[0, 0], wb.at[:, pl.ds(0, 128), pl.ds(0, 128)]),
        (bi.at[0, 0], wb.at[:, pl.ds(128, 128), pl.ds(128, 128)]),
        (bi.at[1, 0], wb.at[:, pl.ds(0, 128), pl.ds(128, 128)]),
    ))]
    for c in loads + more:
        c.start()

    def peer(o):
        return lax.rem(my_y + o // 4, 4) * 4 + lax.rem(my_x + o % 4, 4)

    def copy_a(d, to, slot):
        return pltpu.make_async_remote_copy(
            sa.at[d, to], ra.at[d, slot], a_ss.at[d, to], a_rs.at[d, slot],
            device_id={"rows": to}, device_id_type=MESH)

    def copy_e(d, to, slot):
        return pltpu.make_async_remote_copy(
            se.at[d, to], re_.at[d, slot], e_ss.at[d, to], e_rs.at[d, slot],
            device_id={"rows": to}, device_id_type=MESH)

    def copy_h(d, to, slot):
        return pltpu.make_async_remote_copy(
            sh.at[d, to], rh.at[d, slot], h_ss.at[d, to], h_rs.at[d, slot],
            device_id={"rows": to}, device_id_type=MESH)

    def copy_ia(d):
        return pltpu.make_async_remote_copy(
            ia_s.at[d], ia_r.at[d], ia_sem.at[0, d], ia_sem.at[1, d],
            device_id={"freq": partner}, device_id_type=MESH)

    def copy_ib(d, to, slot):
        return pltpu.make_async_remote_copy(
            ib_s.at[d, to], ib_r.at[d, slot], ib_ss.at[d, to], ib_rs.at[d, slot],
            device_id={"freq": to * 2 + core}, device_id_type=MESH)

    def copy_q(d):
        return pltpu.make_async_remote_copy(
            qq.at[d], qp.at[d], q_sem.at[0, d], q_sem.at[1, d],
            device_id={"freq": partner}, device_id_type=MESH)

    def copy_d(to, slot):
        return pltpu.make_async_remote_copy(
            en_s, en_r.at[slot], d_ss.at[to], d_rs.at[slot],
            device_id={"rows": to}, device_id_type=MESH)

    def copy_t(to, slot):
        return pltpu.make_async_remote_copy(
            et_s, et_r.at[slot], t_ss.at[to], t_rs.at[slot],
            device_id={"freq": to}, device_id_type=MESH)

    def x_radix():
        def rows(c, _):
            r = pl.ds(pl.multiple_of(c * 16, 16), 16)
            ys = fft16([(field[a, r, 0:128], field[a, r, 128:256]) for a in range(16)], -1)
            for k in range(16):
                xb[k, r, 0:128] = ys[k][0].astype(BF16)
                xb[k, r, 128:256] = ys[k][1].astype(BF16)
            return 0

        lax.fori_loop(0, 4, rows, 0)

    def x_block(k):
        return jnp.dot(xb[k], tx[k], preferred_element_type=F32).astype(BF16)

    def x_send(d):
        ra[d, me] = x_block(me)
        for first in range(1, 16, 5):
            for o in range(first, first + 5):
                sa[d, peer(o)] = x_block(peer(o))
            for o in range(first, first + 5):
                copy_a(d, peer(o), me).start()

    def propagator(d):
        omega = fr[0] * sl[d]
        omega2 = omega * omega

        def rows(c, _):
            k1, base = c // 16, lax.rem(c, 16) * 16
            ky = k1 + 4 * (base + lax.broadcasted_iota(jnp.int32, (16, 128), 0))
            kx = me + 16 * lax.broadcasted_iota(jnp.int32, (16, 128), 1)
            ky = jnp.where(2 * ky < NY, ky, ky - NY).astype(F32) * (2.0 * math.pi / NY)
            kx = jnp.where(2 * kx < NX, kx, kx - NX).astype(F32) * (2.0 * math.pi / NX)
            q = omega2 - ky * ky - kx * kx
            root = jnp.sqrt(jnp.abs(q))
            s, co = sin_cos(root)
            up = q >= 0.0
            r = pl.ds(pl.multiple_of(base, 16), 16)
            uu[k1, r, 0:128] = jnp.where(up, co, jnp.exp(-root))
            uu[k1, r, 128:256] = jnp.where(up, s, 0.0)
            return 0

        lax.fori_loop(0, 64, rows, 0)

    def y_radix(d):
        def group(j, _):
            for a in range(4):
                @pl.when(4 * a + j != me)
                def _():
                    copy_a(d, me, 4 * a + j).wait_recv()

            def rows(c, _):
                r = pl.ds(pl.multiple_of(c * 16, 16), 16)
                ys = fft4([
                    (ra[d, 4 * a + j, r, 0:128].astype(F32), ra[d, 4 * a + j, r, 128:256].astype(F32))
                    for a in range(4)], -1)
                o = pl.ds(pl.multiple_of(j * 64 + c * 16, 16), 16)
                for k in range(4):
                    yb[k, o, 0:128] = ys[k][0].astype(BF16)
                    yb[k, o, 128:256] = ys[k][1].astype(BF16)
                return 0

            lax.fori_loop(0, 4, rows, 0)
            return 0

        lax.fori_loop(0, 4, group, 0)

    def y_spectrum():
        for k in range(4):
            cc[k] = jnp.dot(ty[k], yb[k], preferred_element_type=F32)

            def rows(c, _):
                r = pl.ds(pl.multiple_of(c * 16, 16), 16)
                r2 = pl.ds(pl.multiple_of(256 + c * 16, 16), 16)
                br = cc[k, r, 0:128] - cc[k, r2, 128:256]
                bm = cc[k, r, 128:256] + cc[k, r2, 0:128]
                ur, um = uu[k, r, 0:128], uu[k, r, 128:256]
                cb[k, r, 0:128] = (br * ur - bm * um).astype(BF16)
                cb[k, r, 128:256] = (br * um + bm * ur).astype(BF16)
                return 0

            lax.fori_loop(0, 16, rows, 0)

    def y_back(d):
        for k in range(4):
            gg[k] = jnp.dot(tyi[k], cb[k], preferred_element_type=F32)
        for j in range(4):
            for c in range(4):
                r = pl.ds(j * 64 + c * 16, 16)
                r2 = pl.ds(256 + j * 64 + c * 16, 16)
                es = fft4([
                    (gg[k, r, 0:128] - gg[k, r2, 128:256], gg[k, r, 128:256] + gg[k, r2, 0:128])
                    for k in range(4)], 1)
                for a in range(4):
                    s = 4 * a + j
                    for p in range(2):
                        lanes = slice(128 * p, 128 * p + 128)
                        se[d, s, 16 * c:16 * c + 16, lanes] = es[a][p].astype(BF16)
                        if c == 0 and s > 0:
                            sh[d, s - 1, 1:2, lanes] = es[a][p][0:1]
                        if c == 3 and s < 15:
                            sh[d, s + 1, 0:1, lanes] = es[a][p][15:16]
        zero = jnp.zeros((1, 256), F32)
        sh[d, 0, 0:1, :] = zero
        sh[d, 15, 1:2, :] = zero
        re_[d, me] = se[d, me]
        rh[d, me] = sh[d, me]
        for o in range(1, 16):
            copy_e(d, peer(o), me).start()
            copy_h(d, peer(o), me).start()

    def x_back(d):
        for o in range(16):
            k = peer(o)
            if o:
                copy_e(d, me, k).wait_recv()
                copy_h(d, me, k).wait_recv()
            rows = jnp.concatenate(
                [re_[d, k], jnp.concatenate([rh[d, k], jnp.zeros((14, 256), F32)], 0).astype(BF16)], 0)
            gx[k] = jnp.dot(rows, txi[k], preferred_element_type=F32)

        def rows(c, _):
            r = pl.ds(pl.multiple_of(c * 16, 16), 16)
            ss = fft16([(gx[k, r, 0:128], gx[k, r, 128:256]) for k in range(16)], 1)
            o = pl.ds(pl.multiple_of(8 + c * 16, 8), 16)
            for a in range(16):
                sp[a, o, 0:128] = ss[a][0]
                sp[a, o, 128:256] = ss[a][1]
            return 0

        lax.fori_loop(0, 4, rows, 0)
        ss = fft16([(gx[k, 64:72, 0:128], gx[k, 64:72, 128:256]) for k in range(16)], 1)
        for a in range(16):
            for p in range(2):
                sp[a, 7:8, 128 * p:128 * p + 128] = ss[a][p][0:1]
                sp[a, 72:73, 128 * p:128 * p + 128] = ss[a][p][1:2]

    def correct(d):
        gr, gi = cf[0, 0], cf[1, 0]
        for b in range(16):
            s0, lo, hi = sp[b, 8:72, :], sp[b, 7:71, :], sp[b, 9:73, :]
            curve = hi - 2.0 * s0 + lo
            cl, ci = curve[:, 0:128], curve[:, 128:256]
            co = coef[:, 128 * b:128 * b + 128].astype(F32)
            rr = s0[:, 0:128] + co * (gr * cl - gi * ci)
            ri = s0[:, 128:256] + co * (gr * ci + gi * cl)
            r = jnp.concatenate([rr, ri], 1)
            field[b] = r + jnp.dot(r.astype(BF16), wb[b], preferred_element_type=F32)
            if d == DEPTHS - 1:
                for part in range(2):
                    store(b, part).start()
        half = pl.ds(pl.multiple_of(32 * (1 - core), 32), 32)
        for b in range(16):
            ia_s[d, b] = field[b, half, 0:128].astype(BF16)
        copy_ia(d).start()

    def store(b, part):
        return pltpu.make_async_copy(
            field.at[b, :, pl.ds(128 * part, 128)],
            fin.at[part, 0, :, pl.ds(128 * b, 128)], out_sem.at[part, b])

    def chip_sums(d):
        copy_ia(d).wait_recv()
        half = pl.ds(pl.multiple_of(32 * core, 32), 32)
        for b in range(16):
            ib_s[d, b] = (field[b, half, 0:128] + ia_r[d, b].astype(F32)).astype(BF16)
        ib_r[d, chip] = ib_s[d, chip]

        def send(o, _):
            step = jnp.where(lax.rem(o, 2) == 1, 8 - o // 2, 8 + o // 2)
            copy_ib(d, lax.rem(chip + step, CHIPS), chip).start()
            return 0

        lax.fori_loop(1, CHIPS, send, 0)

    def image_sums(d):
        def arrived(o, _):
            copy_ib(d, chip, lax.rem(chip + o, CHIPS)).wait_recv()
            return 0

        lax.fori_loop(1, CHIPS, arrived, 0)
        total = ib_r[d, 0].astype(F32)
        for z in range(1, CHIPS):
            total = total + ib_r[d, z].astype(F32)
        qq[d] = total
        en_s[d:d + 1, :] = jnp.sum(total * total, axis=0, keepdims=True)
        copy_q(d).start()

    def finish():
        en_r[me] = en_s[...]
        for o in range(1, 16):
            copy_d(peer(o), me).start()
        for o in range(1, 16):
            copy_d(me, peer(o)).wait_recv()
        total = en_r[0]
        for k in range(1, 16):
            total = total + en_r[k]
        et_s[...] = total
        et_r[fq] = total

        def send(o, _):
            step = jnp.where(lax.rem(o, 2) == 1, 16 - o // 2, 16 + o // 2)
            copy_t(lax.rem(fq + step, FREQ), fq).start()
            return 0

        lax.fori_loop(1, FREQ, send, 0)

        def arrived(o, _):
            copy_t(fq, lax.rem(fq + o, FREQ)).wait_recv()
            return 0

        lax.fori_loop(1, FREQ, arrived, 0)
        total = et_r[0]
        for k in range(1, FREQ):
            total = total + et_r[k]
        for d in range(DEPTHS):
            copy_q(d).wait_recv()
            energy = jnp.sum(total[d:d + 1, :], axis=1, keepdims=True)
            scale = lax.rsqrt(energy / (NX * NY) + EPS)
            for rows, got in ((core, qq[d]), (1 - core, qp[d])):
                mine = jnp.where(core == 0, got[:, 0:64], got[:, 64:128])
                img[d, pl.ds(pl.multiple_of(32 * rows, 32), 32), :] = mine * scale

    for c in loads:
        c.wait()
    x_radix()
    more[0].wait()
    pl.semaphore_wait(barrier, ROWS + FREQ - 2)
    for d in range(DEPTHS):
        if d:
            x_radix()
        x_send(d)
        propagator(d)
        if d == 0:
            for c in more[1:]:
                c.wait()
            for b in range(16):
                wb[b, 128:256, 0:128] = -wb[b, 0:128, 128:256]
        else:
            chip_sums(0)
        y_radix(d)
        y_spectrum()
        y_back(d)
        if d:
            image_sums(0)
        x_back(d)
        correct(d)
    chip_sums(1)
    image_sums(1)
    finish()

    for b in range(16):
        for part in range(2):
            store(b, part).wait()
    for d in range(DEPTHS):
        copy_ia(d).wait_send()
        copy_q(d).wait_send()

        def sent(o, _):
            to = lax.rem(me + o, ROWS)
            copy_a(d, to, me).wait_send()
            copy_e(d, to, me).wait_send()
            copy_h(d, to, me).wait_send()
            copy_ib(d, lax.rem(chip + o, CHIPS), chip).wait_send()
            return 0

        lax.fori_loop(1, ROWS, sent, 0)

    def sent_d(o, _):
        copy_d(lax.rem(me + o, ROWS), me).wait_send()
        return 0

    def sent_t(o, _):
        copy_t(lax.rem(fq + o, FREQ), fq).wait_send()
        return 0

    lax.fori_loop(1, ROWS, sent_d, 0)
    lax.fori_loop(1, FREQ, sent_t, 0)


def shards(wavefield, block_inverse, coefficient, correction_factor, frequencies, slowness):
    tabs = [jnp.asarray(t, BF16) for t in tables()]
    anywhere = pl.BlockSpec(memory_space=pl.ANY)
    vmem = pl.BlockSpec(memory_space=pltpu.VMEM)
    smem = pl.BlockSpec(memory_space=pltpu.SMEM)
    dma = pltpu.SemaphoreType.DMA
    v = pltpu.VMEM
    scratch = [
        v((16, 64, 256), F32),
        v((16, 256, 256), BF16),
        v((16, 256, 256), BF16),
        v((4, 512, 256), BF16),
        v((4, 512, 256), BF16),
        v((16, 256, 256), BF16),
        v((16, 64, 256), BF16),
        v((2, 16, 64, 256), BF16),
        v((2, 16, 64, 256), BF16),
        v((4, 256, 256), BF16),
        v((4, 512, 256), F32),
        v((4, 256, 256), F32),
        v((4, 256, 256), BF16),
        v((4, 512, 256), F32),
        v((2, 16, 64, 256), BF16),
        v((2, 16, 64, 256), BF16),
        v((2, 16, 2, 256), F32),
        v((2, 16, 2, 256), F32),
        v((16, 80, 256), F32),
        v((16, 80, 256), F32),
        v((2, 16, 32, 128), BF16),
        v((2, 16, 32, 128), BF16),
        v((2, 16, 32, 128), BF16),
        v((2, 16, 32, 128), BF16),
        v((2, 32, 128), F32),
        v((2, 32, 128), F32),
        v((2, 128), F32),
        v((16, 2, 128), F32),
        v((2, 128), F32),
        v((32, 2, 128), F32),
        dma((2, 16)), dma((7,)),
        dma((2, 16)), dma((2, 16)), dma((2, 16)), dma((2, 16)), dma((2, 16)), dma((2, 16)),
        dma((2, 2)), dma((2, 16)), dma((2, 16)), dma((2, 2)),
        dma((16,)), dma((16,)), dma((32,)), dma((32,)), dma((2, 16)),
    ]
    return pl.pallas_call(
        kernel,
        out_shape=(
            jax.ShapeDtypeStruct((2, 64, 64), F32),
            jax.ShapeDtypeStruct((2, 1, 64, 2048), F32),
        ),
        in_specs=[anywhere, anywhere, vmem, smem, smem, smem] + [anywhere] * 4,
        out_specs=(vmem, anywhere),
        scratch_shapes=scratch,
        compiler_params=pltpu.CompilerParams(
            collective_id=0, has_side_effects=True, vmem_limit_bytes=56 << 20),
    )(wavefield, block_inverse, coefficient, correction_factor, frequencies, slowness, *tabs)


def solution(mesh):
    placed = (
        P(None, "freq", "rows", None),
        P(None, "freq", None, None, None),
        P("rows", None),
        P(None, "freq"),
        P("freq"),
        P(),
    )
    return jax.shard_map(
        shards,
        mesh=mesh,
        in_specs=placed,
        out_specs=(P(None, "rows", "freq"), P(None, "freq", "rows", None)),
        check_vma=False,
    )
```

```python
import math

import jax
import jax.numpy as jnp
import numpy as np
from jax import lax
from jax.experimental import pallas as pl
from jax.experimental.pallas import tpu as pltpu
from jax.sharding import PartitionSpec as P

MESH = pl.DeviceIdType.MESH
F32 = jnp.float32
BF16 = jnp.bfloat16
NX = 2048
NY = 1024
DEPTHS = 2
ROWS = 16
FREQ = 32
CHIPS = 16
EPS = 1e-06
EDGES = [0, 63, 64, 127, 128, 191, 192, 255]
FAR = sorted(
    [(dy, dx) for dy in range(4) for dx in range(4) if dy or dx],
    key=lambda o: -(min(o[0], 4 - o[0]) + min(o[1], 4 - o[1])))
SIDES = (2, 1, 3, 0)


def tables():
    b, k2 = np.arange(128)[:, None], np.arange(128)[None, :]
    fwd, inv = [], []
    for k1 in range(16):
        angle = -2.0 * np.pi * ((b * (k1 + 16 * k2)) % NX) / NX
        re, im = np.cos(angle), np.sin(angle)
        block = np.block([[re, im], [-im, re]])
        fwd.append(block)
        inv.append(block.T / NX)
    k2, b = np.arange(256)[:, None], np.arange(256)[None, :]
    yfwd, yinv = [], []
    for k1 in range(4):
        angle = -2.0 * np.pi * ((b * (k1 + 4 * k2)) % NY) / NY
        re, im = np.cos(angle), np.sin(angle)
        yfwd.append([np.concatenate([re[64 * m:64 * m + 64], im[64 * m:64 * m + 64]], 0) for m in range(4)])
        re, im = re.T / NY, -im.T / NY
        rows = [part[64 * j:64 * j + 64] for j in range(4) for part in (re, im)]
        yinv.append(np.concatenate(rows + [re[EDGES], im[EDGES]], 0))
    return [np.stack(t).astype(np.float32) for t in (fwd, inv, yfwd, yinv)]


def add(p, q):
    return p[0] + q[0], p[1] + q[1]


def sub(p, q):
    return p[0] - q[0], p[1] - q[1]


def fft4(x, sign):
    a, b = add(x[0], x[2]), sub(x[0], x[2])
    c, d = add(x[1], x[3]), sub(x[1], x[3])
    turned = (-sign * d[1], sign * d[0]) if sign > 0 else (d[1], -d[0])
    return [add(a, c), add(b, turned), sub(a, c), sub(b, turned)]


def twist(p, m, sign):
    re, im = p
    if m == 0:
        return p
    if m == 4:
        return (-im, re) if sign > 0 else (im, -re)
    if m == 2:
        h = math.sqrt(0.5)
        return ((re - im) * h, (re + im) * h) if sign > 0 else ((re + im) * h, (im - re) * h)
    c, s = math.cos(2 * math.pi * m / 16), sign * math.sin(2 * math.pi * m / 16)
    return re * c - im * s, re * s + im * c


def fft16(x, sign):
    inner = [fft4([x[4 * n1 + n2] for n1 in range(4)], sign) for n2 in range(4)]
    out = [None] * 16
    for k1 in range(4):
        got = fft4([twist(inner[n2][k1], n2 * k1, sign) for n2 in range(4)], sign)
        for k2 in range(4):
            out[k1 + 4 * k2] = got[k2]
    return out


def sin_cos(r):
    n = jnp.floor(r * (2.0 / math.pi) + 0.5)
    t = (r - n * 1.5703125) - n * (math.pi / 2 - 1.5703125)
    t2 = t * t
    sine = t + t * t2 * (-1 / 6 + t2 * (1 / 120 + t2 * (-1 / 5040 + t2 * (1 / 362880))))
    cosine = 1.0 + t2 * (-0.5 + t2 * (1 / 24 + t2 * (-1 / 720 + t2 * (1 / 40320))))
    m = n - 4.0 * jnp.floor(n * 0.25)
    odd = (m == 1.0) | (m == 3.0)
    s, c = jnp.where(odd, cosine, sine), jnp.where(odd, sine, cosine)
    return jnp.where(m >= 2.0, -s, s), jnp.where((m == 1.0) | (m == 2.0), -c, c)


def kernel(
    wf, bi, coef_h, scalars, tx_h, txi_h, ty_h, tyi_h,
    img, fin,
    field, coef, tx, txi, ty, tyi, wb, xb, sa, ra, yb, uu, cb, gg, gh, se, re_, sh, rh, gx, sp, spare,
    ia_s, ia_r, ib_s, ib_r, qq, qp, en_s, en_r, et_s, et_r,
    in_sem, tab_sem, a_ss, a_rs, e_ss, e_rs, h_ss, h_rs, ia_sem, ib_ss, ib_rs, q_sem,
    d_ss, d_rs, t_ss, t_rs, out_sem, up_sem, down_sem,
):
    me = lax.axis_index("rows")
    fq = lax.axis_index("freq")
    my_y, my_x = me // 4, lax.rem(me, 4)
    chip, core = fq // 2, lax.rem(fq, 2)
    partner = chip * 2 + (1 - core)

    barrier = pltpu.get_barrier_semaphore()

    def greet_rows(o, _):
        pl.semaphore_signal(barrier, inc=1, device_id={"rows": lax.rem(me + o, ROWS)}, device_id_type=MESH)
        return 0

    lax.fori_loop(1, ROWS, greet_rows, 0)
    above = lax.rem(chip + 1, CHIPS) * 2 + core
    below = lax.rem(chip + CHIPS - 1, CHIPS) * 2 + core
    for to in (partner, above, below):
        pl.semaphore_signal(barrier, inc=1, device_id={"freq": to}, device_id_type=MESH)

    def relay(wait=True, signal=True):
        if wait:
            pl.semaphore_wait(up_sem, 1)
            pl.semaphore_wait(down_sem, 1)
        if signal:
            pl.semaphore_signal(up_sem, inc=1, device_id={"freq": above}, device_id_type=MESH)
            pl.semaphore_signal(down_sem, inc=1, device_id={"freq": below}, device_id_type=MESH)

    loads = []
    for part in range(2):
        for a in range(16):
            loads.append(pltpu.make_async_copy(
                wf.at[part, 0, :, pl.ds(128 * a, 128)],
                field.at[a, :, pl.ds(128 * part, 128)], in_sem))
    more = [pltpu.make_async_copy(s, d, tab_sem.at[i]) for i, (s, d) in enumerate((
        (tx_h, tx), (ty_h, ty), (tyi_h, tyi), (txi_h, txi), (coef_h, coef),
        (bi.at[0, 0], wb.at[:, pl.ds(0, 128), pl.ds(0, 128)]),
        (bi.at[0, 0], wb.at[:, pl.ds(128, 128), pl.ds(128, 128)]),
        (bi.at[1, 0], wb.at[:, pl.ds(0, 128), pl.ds(128, 128)]),
    ))]
    for c in loads + more:
        c.start()

    def peer(o):
        return lax.rem(my_y + o[0], 4) * 4 + lax.rem(my_x + o[1], 4)

    def source(o):
        return peer((4 - o[0], 4 - o[1]))

    def copy_a(d, o):
        return pltpu.make_async_remote_copy(
            sa.at[d, peer(o)], ra.at[d, me], a_ss.at[d], a_rs.at[d, o[1]],
            device_id={"rows": peer(o)}, device_id_type=MESH)

    def copy_e(d, o):
        return pltpu.make_async_remote_copy(
            se.at[d, peer(o)], re_.at[d, me], e_ss.at[d], e_rs.at[d, o[1]],
            device_id={"rows": peer(o)}, device_id_type=MESH)

    def copy_h(d, o):
        return pltpu.make_async_remote_copy(
            sh.at[d, peer(o)], rh.at[d, me], h_ss.at[d], h_rs.at[d],
            device_id={"rows": peer(o)}, device_id_type=MESH)

    def copy_ia(d):
        return pltpu.make_async_remote_copy(
            ia_s.at[d], ia_r.at[d], ia_sem.at[0, d], ia_sem.at[1, d],
            device_id={"freq": partner}, device_id_type=MESH)

    def copy_ib(d, to):
        return pltpu.make_async_remote_copy(
            ib_s.at[d, to], ib_r.at[d, chip], ib_ss.at[d], ib_rs.at[d],
            device_id={"freq": to * 2 + core}, device_id_type=MESH)

    def copy_q(d):
        return pltpu.make_async_remote_copy(
            qq.at[d], qp.at[d], q_sem.at[0, d], q_sem.at[1, d],
            device_id={"freq": partner}, device_id_type=MESH)

    def copy_d(o):
        return pltpu.make_async_remote_copy(
            en_s, en_r.at[me], d_ss, d_rs,
            device_id={"rows": peer(o)}, device_id_type=MESH)

    def copy_t(to):
        return pltpu.make_async_remote_copy(
            et_s, et_r.at[fq], t_ss, t_rs,
            device_id={"freq": to}, device_id_type=MESH)

    def bytes_of(ref, sem):
        pltpu.make_async_copy(ref, ref, sem).wait()

    def x_radix():
        def rows(c, _):
            r = pl.ds(pl.multiple_of(c * 16, 16), 16)
            ys = fft16([(field[a, r, 0:128], field[a, r, 128:256]) for a in range(16)], -1)
            for k in range(16):
                xb[k, r, 0:128] = ys[k][0].astype(BF16)
                xb[k, r, 128:256] = ys[k][1].astype(BF16)
            return 0

        lax.fori_loop(0, 4, rows, 0)

    def x_block(k):
        return jnp.dot(xb[k], tx[k], preferred_element_type=F32).astype(BF16)

    def x_fill(d, some):
        for o in some:
            sa[d, peer(o)] = x_block(peer(o))

    def x_start(d, some):
        for o in some:
            copy_a(d, o).start()

    def propagator(d):
        omega = scalars[2] * scalars[3 + d]
        omega2 = omega * omega

        def rows(c, _):
            k1, base = c // 16, lax.rem(c, 16) * 16
            ky = k1 + 4 * (base + lax.broadcasted_iota(jnp.int32, (16, 128), 0))
            kx = me + 16 * lax.broadcasted_iota(jnp.int32, (16, 128), 1)
            ky = jnp.where(2 * ky < NY, ky, ky - NY).astype(F32) * (2.0 * math.pi / NY)
            kx = jnp.where(2 * kx < NX, kx, kx - NX).astype(F32) * (2.0 * math.pi / NX)
            q = omega2 - ky * ky - kx * kx
            root = jnp.sqrt(jnp.abs(q))
            s, co = sin_cos(root)
            up = q >= 0.0
            r = pl.ds(pl.multiple_of(base, 16), 16)
            uu[k1, r, 0:128] = jnp.where(up, co, jnp.exp(-root))
            uu[k1, r, 128:256] = jnp.where(up, s, 0.0)
            return 0

        lax.fori_loop(0, 64, rows, 0)

    def y_radix(d):
        for dx in SIDES:
            j = lax.rem(my_x + 4 - dx, 4)
            bytes_of(ra.at[d, 0:4 if dx else 3], a_rs.at[d, dx])

            def rows(c, _):
                r = pl.ds(pl.multiple_of(c * 16, 16), 16)
                ys = fft4([
                    (ra[d, 4 * a + j, r, 0:128].astype(F32), ra[d, 4 * a + j, r, 128:256].astype(F32))
                    for a in range(4)], -1)
                o = pl.ds(pl.multiple_of(j * 64 + c * 16, 16), 16)
                for k in range(4):
                    yb[k, o, 0:128] = ys[k][0].astype(BF16)
                    yb[k, o, 128:256] = ys[k][1].astype(BF16)
                return 0

            lax.fori_loop(0, 4, rows, 0)

    def y_spectrum():
        for k in range(4):
            for m in range(4):
                got = jnp.dot(ty[k, m], yb[k], preferred_element_type=F32)
                top, low = got[0:64], got[64:128]
                br = top[:, 0:128] - low[:, 128:256]
                bm = top[:, 128:256] + low[:, 0:128]
                r = slice(64 * m, 64 * m + 64)
                ur, um = uu[k, r, 0:128], uu[k, r, 128:256]
                cb[k, r, 0:128] = (br * ur - bm * um).astype(BF16)
                cb[k, r, 128:256] = (br * um + bm * ur).astype(BF16)

    def y_back(d):
        for k in range(4):
            gh[k] = jnp.dot(tyi[k, 512:528], cb[k], preferred_element_type=F32)
        edge = fft4([
            (gh[k, 0:8, 0:128] - gh[k, 8:16, 128:256], gh[k, 0:8, 128:256] + gh[k, 8:16, 0:128])
            for k in range(4)], 1)
        zero = jnp.zeros((1, 128), F32)
        for s in range(16):
            for p in range(2):
                lanes = slice(128 * p, 128 * p + 128)
                below_a, below_j = divmod(s - 1, 4)
                above_a, above_j = divmod(s + 1, 4)
                sh[d, s, 0:1, lanes] = edge[below_a][p][2 * below_j + 1:2 * below_j + 2] if s else zero
                sh[d, s, 1:2, lanes] = edge[above_a][p][2 * above_j:2 * above_j + 1] if s < 15 else zero
        rh[d, me] = sh[d, me]
        for o in FAR:
            copy_h(d, o).start()
        for dx in SIDES:
            j = lax.rem(my_x + dx, 4)
            for k in range(4):
                gg[dx, k] = jnp.dot(tyi[k, pl.ds(pl.multiple_of(128 * j, 128), 128)], cb[k], preferred_element_type=F32)
            for c in range(4):
                r, r2 = slice(16 * c, 16 * c + 16), slice(64 + 16 * c, 80 + 16 * c)
                es = fft4([
                    (gg[dx, k, r, 0:128] - gg[dx, k, r2, 128:256], gg[dx, k, r, 128:256] + gg[dx, k, r2, 0:128])
                    for k in range(4)], 1)
                for a in range(4):
                    for p in range(2):
                        se[d, 4 * a + j, r, 128 * p:128 * p + 128] = es[a][p].astype(BF16)
            for dy in (2, 1, 3, 0):
                if dx or dy:
                    copy_e(d, (dy, dx)).start()
        re_[d, me] = se[d, me]

    def x_back(d):
        bytes_of(rh.at[d, 0:15], h_rs.at[d])
        for o in [(dy, dx) for dx in SIDES for dy in (2, 1, 3, 0)]:
            k = source(o)
            if o[0] == 2:
                bytes_of(re_.at[d, 0:4 if o[1] else 3], e_rs.at[d, o[1]])
            rows = jnp.concatenate(
                [re_[d, k], jnp.concatenate([rh[d, k], jnp.zeros((14, 256), F32)], 0).astype(BF16)], 0)
            gx[k] = jnp.dot(rows, txi[k], preferred_element_type=F32)

        def rows(c, _):
            r = pl.ds(pl.multiple_of(c * 16, 16), 16)
            ss = fft16([(gx[k, r, 0:128], gx[k, r, 128:256]) for k in range(16)], 1)
            o = pl.ds(pl.multiple_of(8 + c * 16, 8), 16)
            for a in range(16):
                sp[a, o, 0:128] = ss[a][0]
                sp[a, o, 128:256] = ss[a][1]
            return 0

        lax.fori_loop(0, 4, rows, 0)
        ss = fft16([(gx[k, 64:72, 0:128], gx[k, 64:72, 128:256]) for k in range(16)], 1)
        for a in range(16):
            for p in range(2):
                sp[a, 7:8, 128 * p:128 * p + 128] = ss[a][p][0:1]
                sp[a, 72:73, 128 * p:128 * p + 128] = ss[a][p][1:2]

    def correct(d):
        gr, gi = scalars[0], scalars[1]
        for b in range(16):
            s0, lo, hi = sp[b, 8:72, :], sp[b, 7:71, :], sp[b, 9:73, :]
            curve = hi - 2.0 * s0 + lo
            cl, ci = curve[:, 0:128], curve[:, 128:256]
            co = coef[:, 128 * b:128 * b + 128].astype(F32)
            rr = s0[:, 0:128] + co * (gr * cl - gi * ci)
            ri = s0[:, 128:256] + co * (gr * ci + gi * cl)
            r = jnp.concatenate([rr, ri], 1)
            field[b] = r + jnp.dot(r.astype(BF16), wb[b], preferred_element_type=F32)
            if d == DEPTHS - 1 and b % 8 == 7:
                for done in range(b - 7, b + 1):
                    for part in range(2):
                        store(done, part).start()
        half = pl.ds(pl.multiple_of(32 * (1 - core), 32), 32)
        for b in range(16):
            ia_s[d, b] = field[b, half, 0:128].astype(BF16)
        copy_ia(d).start()

    def store(b, part):
        return pltpu.make_async_copy(
            field.at[b, :, pl.ds(128 * part, 128)],
            fin.at[part, 0, :, pl.ds(128 * b, 128)], out_sem)

    def chip_sums(d):
        copy_ia(d).wait_recv()
        half = pl.ds(pl.multiple_of(32 * core, 32), 32)
        for b in range(16):
            ib_s[d, b] = (field[b, half, 0:128] + ia_r[d, b].astype(F32)).astype(BF16)
        ib_r[d, chip] = ib_s[d, chip]

        def send(o, _):
            step = jnp.where(lax.rem(o, 2) == 1, 8 - o // 2, 8 + o // 2)
            copy_ib(d, lax.rem(chip + step, CHIPS)).start()
            return 0

        lax.fori_loop(1, CHIPS, send, 0)

    def image_sums(d):
        bytes_of(ib_r.at[d, 0:15], ib_rs.at[d])
        total = ib_r[d, 0].astype(F32)
        for z in range(1, CHIPS):
            total = total + ib_r[d, z].astype(F32)
        qq[d] = total
        en_s[d:d + 1, :] = jnp.sum(total * total, axis=0, keepdims=True)
        copy_q(d).start()

    def sent(d):
        copy_ia(d).wait_send()
        bytes_of(sa.at[d, 0:15], a_ss.at[d])
        bytes_of(se.at[d, 0:15], e_ss.at[d])
        bytes_of(sh.at[d, 0:15], h_ss.at[d])
        bytes_of(ib_s.at[d, 0:15], ib_ss.at[d])

    def finish():
        en_r[me] = en_s[...]
        for o in FAR:
            copy_d(o).start()
        bytes_of(en_r.at[0:15], d_rs)
        total = en_r[0]
        for k in range(1, 16):
            total = total + en_r[k]
        et_s[...] = total
        et_r[fq] = total

        def send(o, _):
            step = jnp.where(lax.rem(o, 2) == 1, 16 - o // 2, 16 + o // 2)
            copy_t(lax.rem(fq + step, FREQ)).start()
            return 0

        lax.fori_loop(1, FREQ, send, 0)

        bytes_of(et_r.at[0:31], t_rs)
        total = et_r[0]
        for k in range(1, FREQ):
            total = total + et_r[k]
        copy_q(1).wait_send()
        for d in range(DEPTHS):
            copy_q(d).wait_recv()
            energy = jnp.sum(total[d:d + 1, :], axis=1, keepdims=True)
            scale = lax.rsqrt(energy / (NX * NY) + EPS)
            for rows, got in ((core, qq[d]), (1 - core, qp[d])):
                mine = jnp.where(core == 0, got[:, 0:64], got[:, 64:128])
                img[d, pl.ds(pl.multiple_of(32 * rows, 32), 32), :] = mine * scale

    pltpu.make_async_copy(spare, field, in_sem).wait()
    x_radix()
    more[0].wait()
    x_fill(0, FAR)
    pl.semaphore_wait(barrier, ROWS + 2)
    x_start(0, FAR)
    ra[0, me] = x_block(me)
    for d in range(DEPTHS):
        if d:
            x_radix()
            for first in range(0, 15, 5):
                x_fill(d, FAR[first:first + 5])
                x_start(d, FAR[first:first + 5])
            ra[d, me] = x_block(me)
        if d == 0:
            relay(wait=False)
        propagator(d)
        if d == 0:
            relay()
            for c in more[1:]:
                c.wait()
            for b in range(16):
                wb[b, 128:256, 0:128] = -wb[b, 0:128, 128:256]
            relay()
        else:
            relay(signal=False)
            chip_sums(0)
        y_radix(d)
        if d == 0:
            relay()
        y_spectrum()
        if d == 0:
            relay()
        y_back(d)
        if d:
            image_sums(0)
        else:
            relay()
        x_back(d)
        if d == 0:
            relay()
        correct(d)
        if d == 0:
            relay()
    chip_sums(1)
    sent(0)
    sent(1)
    copy_q(0).wait_send()
    image_sums(1)
    finish()

    pltpu.make_async_copy(field, spare, out_sem).wait()

    bytes_of(en_r.at[0:15], d_ss)
    bytes_of(et_r.at[0:31], t_ss)


def shards(wavefield, block_inverse, coefficient, correction_factor, frequencies, slowness):
    tabs = [jnp.asarray(t, BF16) for t in tables()]
    scalars = jnp.concatenate([correction_factor.reshape(2), frequencies, slowness])
    anywhere = pl.BlockSpec(memory_space=pl.ANY)
    hbm = pl.BlockSpec(memory_space=pltpu.HBM)
    vmem = pl.BlockSpec(memory_space=pltpu.VMEM)
    smem = pl.BlockSpec(memory_space=pltpu.SMEM)
    dma = pltpu.SemaphoreType.DMA
    v = pltpu.VMEM
    scratch = [
        v((16, 64, 256), F32),
        v((64, 2048), BF16),
        v((16, 256, 256), BF16),
        v((16, 256, 256), BF16),
        v((4, 4, 128, 256), BF16),
        v((4, 528, 256), BF16),
        v((16, 256, 256), BF16),
        v((16, 64, 256), BF16),
        v((2, 16, 64, 256), BF16),
        v((2, 16, 64, 256), BF16),
        v((4, 256, 256), BF16),
        v((4, 256, 256), F32),
        v((4, 256, 256), BF16),
        v((4, 4, 128, 256), F32),
        v((4, 16, 256), F32),
        v((2, 16, 64, 256), BF16),
        v((2, 16, 64, 256), BF16),
        v((2, 16, 2, 256), F32),
        v((2, 16, 2, 256), F32),
        v((16, 80, 256), F32),
        v((16, 80, 256), F32),
        v((16, 64, 256), F32),
        v((2, 16, 32, 128), BF16),
        v((2, 16, 32, 128), BF16),
        v((2, 16, 32, 128), BF16),
        v((2, 16, 32, 128), BF16),
        v((2, 32, 128), F32),
        v((2, 32, 128), F32),
        v((2, 128), F32),
        v((16, 2, 128), F32),
        v((2, 128), F32),
        v((32, 2, 128), F32),
        dma, dma((8,)),
        dma((2,)), dma((2, 4)), dma((2,)), dma((2, 4)), dma((2,)), dma((2,)),
        dma((2, 2)), dma((2,)), dma((2,)), dma((2, 2)),
        dma, dma, dma, dma, dma,
        pltpu.SemaphoreType.REGULAR, pltpu.SemaphoreType.REGULAR,
    ]
    return pl.pallas_call(
        kernel,
        out_shape=(
            jax.ShapeDtypeStruct((2, 64, 64), F32),
            jax.ShapeDtypeStruct((2, 1, 64, 2048), F32),
        ),
        in_specs=[hbm, hbm, hbm, smem] + [hbm] * 4,
        out_specs=(vmem, anywhere),
        scratch_shapes=scratch,
        compiler_params=pltpu.CompilerParams(
            collective_id=0, has_side_effects=True, vmem_limit_bytes=54525952),
    )(wavefield, block_inverse, coefficient, scalars, *tabs)


def solution(mesh):
    placed = (
        P(None, "freq", "rows", None),
        P(None, "freq", None, None, None),
        P("rows", None),
        P(None, "freq"),
        P("freq"),
        P(),
    )
    return jax.shard_map(
        shards,
        mesh=mesh,
        in_specs=placed,
        out_specs=(P(None, "rows", "freq"), P(None, "freq", "rows", None)),
        check_vma=False,
    )
```

```python
import math

import jax
import jax.numpy as jnp
import numpy as np
from jax import lax
from jax.experimental import pallas as pl
from jax.experimental.pallas import tpu as pltpu
from jax.sharding import PartitionSpec as P

MESH = pl.DeviceIdType.MESH
F32 = jnp.float32
BF16 = jnp.bfloat16
NX = 2048
NY = 1024
DEPTHS = 2
ROWS = 16
FREQ = 32
CHIPS = 16
EPS = 1e-06
EDGES = [64 * j + r for j in range(4) for r in (0, 31, 32, 63)]
FAR = sorted(
    [(dy, dx) for dy in range(4) for dx in range(4) if dy or dx],
    key=lambda o: -(min(o[0], 4 - o[0]) + min(o[1], 4 - o[1])))
SIDES = (2, 1, 3, 0)


def tables():
    b, k2 = np.arange(128)[:, None], np.arange(128)[None, :]
    fwd, inv = [], []
    for k1 in range(16):
        angle = -2.0 * np.pi * ((b * (k1 + 16 * k2)) % NX) / NX
        re, im = np.cos(angle), np.sin(angle)
        block = np.block([[re, im], [-im, re]])
        fwd.append(block)
        inv.append(block.T / NX)
    k2, b = np.arange(256)[:, None], np.arange(256)[None, :]
    yfwd, yinv = [], []
    for k1 in range(4):
        angle = -2.0 * np.pi * ((b * (k1 + 4 * k2)) % NY) / NY
        re, im = np.cos(angle), np.sin(angle)
        yfwd.append([np.concatenate([re[64 * m:64 * m + 64], im[64 * m:64 * m + 64]], 0) for m in range(4)])
        re, im = re.T / NY, -im.T / NY
        rows = [part[64 * j:64 * j + 64] for j in range(4) for part in (re, im)]
        yinv.append(np.concatenate(rows + [re[EDGES], im[EDGES]], 0))
    return [np.stack(t).astype(np.float32) for t in (fwd, inv, yfwd, yinv)]


def add(p, q):
    return p[0] + q[0], p[1] + q[1]


def sub(p, q):
    return p[0] - q[0], p[1] - q[1]


def fft4(x, sign):
    a, b = add(x[0], x[2]), sub(x[0], x[2])
    c, d = add(x[1], x[3]), sub(x[1], x[3])
    turned = (-sign * d[1], sign * d[0]) if sign > 0 else (d[1], -d[0])
    return [add(a, c), add(b, turned), sub(a, c), sub(b, turned)]


def twist(p, m, sign):
    re, im = p
    if m == 0:
        return p
    if m == 4:
        return (-im, re) if sign > 0 else (im, -re)
    if m == 2:
        h = math.sqrt(0.5)
        return ((re - im) * h, (re + im) * h) if sign > 0 else ((re + im) * h, (im - re) * h)
    c, s = math.cos(2 * math.pi * m / 16), sign * math.sin(2 * math.pi * m / 16)
    return re * c - im * s, re * s + im * c


def fft16(x, sign):
    inner = [fft4([x[4 * n1 + n2] for n1 in range(4)], sign) for n2 in range(4)]
    out = [None] * 16
    for k1 in range(4):
        got = fft4([twist(inner[n2][k1], n2 * k1, sign) for n2 in range(4)], sign)
        for k2 in range(4):
            out[k1 + 4 * k2] = got[k2]
    return out


def sin_cos(r):
    n = jnp.floor(r * (2.0 / math.pi) + 0.5)
    t = (r - n * 1.5703125) - n * (math.pi / 2 - 1.5703125)
    t2 = t * t
    sine = t + t * t2 * (-1 / 6 + t2 * (1 / 120 + t2 * (-1 / 5040 + t2 * (1 / 362880))))
    cosine = 1.0 + t2 * (-0.5 + t2 * (1 / 24 + t2 * (-1 / 720 + t2 * (1 / 40320))))
    m = n - 4.0 * jnp.floor(n * 0.25)
    odd = (m == 1.0) | (m == 3.0)
    s, c = jnp.where(odd, cosine, sine), jnp.where(odd, sine, cosine)
    return jnp.where(m >= 2.0, -s, s), jnp.where((m == 1.0) | (m == 2.0), -c, c)


def kernel(
    wf, bi, coef_h, scalars, tx_h, txi_h, ty_h, tyi_h,
    img, fin,
    field, coef, tx, txi, ty, tyi, wb, xb, sa, ra, yb, uu, cb, gg, gh, se, re_, sh, rh, gx, sp, spare,
    ia_s, ia_r, ib_s, ib_r, qq, qp, en_s, en_r, et_s, et_r,
    in_sem, tab_sem, a_ss, a_rs, e_ss, e_rs, h_ss, h_rs, ia_sem, ib_ss, ib_rs, q_sem,
    d_ss, d_rs, t_ss, t_rs, out_sem, up_sem, down_sem,
):
    me = lax.axis_index("rows")
    fq = lax.axis_index("freq")
    my_y, my_x = me // 4, lax.rem(me, 4)
    chip, core = fq // 2, lax.rem(fq, 2)
    partner = chip * 2 + (1 - core)

    barrier = pltpu.get_barrier_semaphore()

    def greet_rows(o, _):
        pl.semaphore_signal(barrier, inc=1, device_id={"rows": lax.rem(me + o, ROWS)}, device_id_type=MESH)
        return 0

    lax.fori_loop(1, ROWS, greet_rows, 0)
    above = lax.rem(chip + 1, CHIPS) * 2 + core
    below = lax.rem(chip + CHIPS - 1, CHIPS) * 2 + core
    for to in (partner, above, below):
        pl.semaphore_signal(barrier, inc=1, device_id={"freq": to}, device_id_type=MESH)

    def relay(wait=True, signal=True):
        if wait:
            pl.semaphore_wait(up_sem, 1)
            pl.semaphore_wait(down_sem, 1)
        if signal:
            pl.semaphore_signal(up_sem, inc=1, device_id={"freq": above}, device_id_type=MESH)
            pl.semaphore_signal(down_sem, inc=1, device_id={"freq": below}, device_id_type=MESH)

    loads = []
    for h in range(2):
        rows = pl.ds(32 * h, 32)
        for part in range(2):
            for a in range(16):
                loads.append(pltpu.make_async_copy(
                    wf.at[part, 0, rows, pl.ds(128 * a, 128)],
                    field.at[a, rows, pl.ds(128 * part, 128)], in_sem.at[h]))
    more = [pltpu.make_async_copy(s, d, tab_sem.at[i]) for i, (s, d) in enumerate((
        (tx_h, tx), (ty_h, ty), (tyi_h, tyi), (txi_h, txi), (coef_h, coef),
        (bi.at[0, 0], wb.at[:, pl.ds(0, 128), pl.ds(0, 128)]),
        (bi.at[0, 0], wb.at[:, pl.ds(128, 128), pl.ds(128, 128)]),
        (bi.at[1, 0], wb.at[:, pl.ds(0, 128), pl.ds(128, 128)]),
    ))]
    for c in loads[:32] + more[:1] + loads[32:] + more[1:]:
        c.start()

    def peer(o):
        return lax.rem(my_y + o[0], 4) * 4 + lax.rem(my_x + o[1], 4)

    def source(o):
        return peer((4 - o[0], 4 - o[1]))

    def copy_a(d, o, first, count):
        rows = pl.ds(first, count)
        return pltpu.make_async_remote_copy(
            sa.at[d, peer(o), rows], ra.at[d, me, rows], a_ss.at[d], a_rs.at[d, o[1]],
            device_id={"rows": peer(o)}, device_id_type=MESH)

    def copy_e(d, o, h):
        rows = pl.ds(32 * h, 32)
        return pltpu.make_async_remote_copy(
            se.at[d, peer(o), rows], re_.at[d, me, rows], e_ss.at[d], e_rs.at[d, h, o[1]],
            device_id={"rows": peer(o)}, device_id_type=MESH)

    def copy_h(d, o):
        return pltpu.make_async_remote_copy(
            sh.at[d, peer(o)], rh.at[d, me], h_ss.at[d], h_rs.at[d],
            device_id={"rows": peer(o)}, device_id_type=MESH)

    def copy_ia(d, h):
        return pltpu.make_async_remote_copy(
            ia_s.at[d, h], ia_r.at[d, h], ia_sem.at[0, d, h], ia_sem.at[1, d, h],
            device_id={"freq": partner}, device_id_type=MESH)

    def copy_ib(d, h, to):
        return pltpu.make_async_remote_copy(
            ib_s.at[d, h, to], ib_r.at[d, h, chip], ib_ss.at[d], ib_rs.at[d, h],
            device_id={"freq": to * 2 + core}, device_id_type=MESH)

    def copy_q(d):
        return pltpu.make_async_remote_copy(
            qq.at[d], qp.at[d], q_sem.at[0, d], q_sem.at[1, d],
            device_id={"freq": partner}, device_id_type=MESH)

    def copy_d(o):
        return pltpu.make_async_remote_copy(
            en_s, en_r.at[me], d_ss, d_rs,
            device_id={"rows": peer(o)}, device_id_type=MESH)

    def copy_t(to):
        return pltpu.make_async_remote_copy(
            et_s, et_r.at[fq], t_ss, t_rs,
            device_id={"freq": to}, device_id_type=MESH)

    def bytes_of(ref, sem):
        pltpu.make_async_copy(ref, ref, sem).wait()

    def x_radix(first, count):
        def rows(c, _):
            r = pl.ds(pl.multiple_of(c * 16, 16), 16)
            ys = fft16([(field[a, r, 0:128], field[a, r, 128:256]) for a in range(16)], -1)
            for k in range(16):
                xb[k, r, 0:128] = ys[k][0].astype(BF16)
                xb[k, r, 128:256] = ys[k][1].astype(BF16)
            return 0

        lax.fori_loop(first // 16, (first + count) // 16, rows, 0)

    def x_block(k, rows):
        return jnp.dot(xb[k, rows], tx[k], preferred_element_type=F32).astype(BF16)

    def x_fill(d, some, first, count):
        rows = slice(first, first + count)
        for o in some:
            sa[d, peer(o), rows] = x_block(peer(o), rows)

    def x_own(d, first, count):
        rows = slice(first, first + count)
        ra[d, me, rows] = x_block(me, rows)

    def x_start(d, some, first, count):
        for o in some:
            copy_a(d, o, first, count).start()

    def x_out(d, h):
        step = 15 if h else 5
        for first in range(0, 15, step):
            x_fill(d, FAR[first:first + step], 32 * h, 32)
            x_start(d, FAR[first:first + step], 32 * h, 32)
        x_own(d, 32 * h, 32)

    def propagator(d):
        omega = scalars[2] * scalars[3 + d]
        omega2 = omega * omega

        def rows(c, _):
            k1, base = c // 16, lax.rem(c, 16) * 16
            ky = k1 + 4 * (base + lax.broadcasted_iota(jnp.int32, (16, 128), 0))
            kx = me + 16 * lax.broadcasted_iota(jnp.int32, (16, 128), 1)
            ky = jnp.where(2 * ky < NY, ky, ky - NY).astype(F32) * (2.0 * math.pi / NY)
            kx = jnp.where(2 * kx < NX, kx, kx - NX).astype(F32) * (2.0 * math.pi / NX)
            q = omega2 - ky * ky - kx * kx
            root = jnp.sqrt(jnp.abs(q))
            s, co = sin_cos(root)
            up = q >= 0.0
            r = pl.ds(pl.multiple_of(base, 16), 16)
            uu[k1, r, 0:128] = jnp.where(up, co, jnp.exp(-root))
            uu[k1, r, 128:256] = jnp.where(up, s, 0.0)
            return 0

        lax.fori_loop(0, 64, rows, 0)

    def y_radix(d):
        for dx in SIDES:
            j = lax.rem(my_x + 4 - dx, 4)
            bytes_of(ra.at[d, 0:4 if dx else 3], a_rs.at[d, dx])

            def rows(c, _):
                r = pl.ds(pl.multiple_of(c * 16, 16), 16)
                ys = fft4([
                    (ra[d, 4 * a + j, r, 0:128].astype(F32), ra[d, 4 * a + j, r, 128:256].astype(F32))
                    for a in range(4)], -1)
                o = pl.ds(pl.multiple_of(j * 64 + c * 16, 16), 16)
                for k in range(4):
                    yb[k, o, 0:128] = ys[k][0].astype(BF16)
                    yb[k, o, 128:256] = ys[k][1].astype(BF16)
                return 0

            lax.fori_loop(0, 4, rows, 0)

    def y_spectrum():
        for k in range(4):
            for m in range(4):
                got = jnp.dot(ty[k, m], yb[k], preferred_element_type=F32)
                top, low = got[0:64], got[64:128]
                br = top[:, 0:128] - low[:, 128:256]
                bm = top[:, 128:256] + low[:, 0:128]
                r = slice(64 * m, 64 * m + 64)
                ur, um = uu[k, r, 0:128], uu[k, r, 128:256]
                cb[k, r, 0:128] = (br * ur - bm * um).astype(BF16)
                cb[k, r, 128:256] = (br * um + bm * ur).astype(BF16)

    def y_back(d):
        def edges():
            for k in range(4):
                gh[k] = jnp.dot(tyi[k, 512:544], cb[k], preferred_element_type=F32)
            edge = fft4([
                (gh[k, 0:16, 0:128] - gh[k, 16:32, 128:256], gh[k, 0:16, 128:256] + gh[k, 16:32, 0:128])
                for k in range(4)], 1)
            zero = jnp.zeros((1, 128), F32)
            for s in range(16):
                for p in range(2):
                    lanes = slice(128 * p, 128 * p + 128)
                    for row, (t, e) in enumerate(((s - 1, 3), (s, 2), (s, 1), (s + 1, 0))):
                        at = 4 * (t % 4) + e
                        sh[d, s, row:row + 1, lanes] = edge[t // 4][p][at:at + 1] if 0 <= t < 16 else zero
            rh[d, me] = sh[d, me]
            for o in FAR:
                copy_h(d, o).start()
        def lines(dx):
            j = lax.rem(my_x + dx, 4)
            for k in range(4):
                gg[dx, k] = jnp.dot(
                    tyi[k, pl.ds(pl.multiple_of(128 * j, 128), 128)], cb[k], preferred_element_type=F32)

        lines(SIDES[0])
        for turn, dx in enumerate(SIDES):
            j = lax.rem(my_x + dx, 4)
            if turn:
                lines(dx)
            for c in range(4):
                r, r2 = slice(16 * c, 16 * c + 16), slice(64 + 16 * c, 80 + 16 * c)
                es = fft4([
                    (gg[dx, k, r, 0:128] - gg[dx, k, r2, 128:256], gg[dx, k, r, 128:256] + gg[dx, k, r2, 0:128])
                    for k in range(4)], 1)
                for a in range(4):
                    for p in range(2):
                        se[d, 4 * a + j, r, 128 * p:128 * p + 128] = es[a][p].astype(BF16)
            for dy in (2, 1, 3, 0):
                if dx or dy:
                    copy_e(d, (dy, dx), 0).start()
            if turn == 0:
                edges()
        re_[d, me] = se[d, me]
        for o in FAR:
            copy_e(d, o, 1).start()

    def x_back(d, h):
        if h == 0:
            bytes_of(rh.at[d, 0:15], h_rs.at[d])
        for o in [(dy, dx) for dx in SIDES for dy in (2, 1, 3, 0)]:
            k = source(o)
            if o[0] == 2:
                bytes_of(re_.at[d, 0:4 if o[1] else 3, 0:32], e_rs.at[d, h, o[1]])
            halo = jnp.concatenate([rh[d, k, 2 * h:2 * h + 2], jnp.zeros((14, 256), F32)], 0)
            rows = jnp.concatenate([re_[d, k, 32 * h:32 * h + 32], halo.astype(BF16)], 0)
            gx[h, k] = jnp.dot(rows, txi[k], preferred_element_type=F32)

        def rows(c, _):
            r = pl.ds(pl.multiple_of(c * 16, 16), 16)
            ss = fft16([(gx[h, k, r, 0:128], gx[h, k, r, 128:256]) for k in range(16)], 1)
            o = pl.ds(pl.multiple_of(8 + c * 16, 8), 16)
            for a in range(16):
                sp[h, a, o, 0:128] = ss[a][0]
                sp[h, a, o, 128:256] = ss[a][1]
            return 0

        lax.fori_loop(0, 2, rows, 0)
        ss = fft16([(gx[h, k, 32:40, 0:128], gx[h, k, 32:40, 128:256]) for k in range(16)], 1)
        for a in range(16):
            for p in range(2):
                sp[h, a, 7:8, 128 * p:128 * p + 128] = ss[a][p][0:1]
                sp[h, a, 40:41, 128 * p:128 * p + 128] = ss[a][p][1:2]

    def correct(d, h):
        gr, gi = scalars[0], scalars[1]
        own = slice(32 * h, 32 * h + 32)
        for b in range(16):
            around = sp[h, b]
            s0 = around[8:40]
            lo = pltpu.roll(around, 1, 0)[8:40]
            hi = pltpu.roll(around, 47, 0)[8:40]
            curve = hi - 2.0 * s0 + lo
            cl, ci = curve[:, 0:128], curve[:, 128:256]
            co = coef[own, 128 * b:128 * b + 128].astype(F32)
            cr, cm = co * gr, co * gi
            rr = s0[:, 0:128] + (cr * cl - cm * ci)
            ri = s0[:, 128:256] + (cr * ci + cm * cl)
            r = jnp.concatenate([rr, ri], 1)
            field[b, own] = r + jnp.dot(r.astype(BF16), wb[b], preferred_element_type=F32)
        half = pl.ds(pl.multiple_of(32 * h + 16 * (1 - core), 16), 16)
        for b in range(16):
            ia_s[d, h, b] = field[b, half, 0:128].astype(BF16)
        copy_ia(d, h).start()
        if d == DEPTHS - 1:
            for b in range(16):
                for part in range(2):
                    store(b, part, h).start()

    def store(b, part, h):
        return pltpu.make_async_copy(
            field.at[b, pl.ds(32 * h, 32), pl.ds(128 * part, 128)],
            fin.at[part, 0, pl.ds(32 * h, 32), pl.ds(128 * b, 128)], out_sem)

    def chip_sums(d, h):
        copy_ia(d, h).wait_recv()
        half = pl.ds(pl.multiple_of(32 * h + 16 * core, 16), 16)
        for b in range(16):
            ib_s[d, h, b] = (field[b, half, 0:128] + ia_r[d, h, b].astype(F32)).astype(BF16)
        ib_r[d, h, chip] = ib_s[d, h, chip]

        def send(o, _):
            step = jnp.where(lax.rem(o, 2) == 1, 8 - o // 2, 8 + o // 2)
            copy_ib(d, h, lax.rem(chip + step, CHIPS)).start()
            return 0

        lax.fori_loop(1, CHIPS, send, 0)

    def image_sums(d):
        squares = jnp.zeros((1, 128), F32)
        for h in range(2):
            bytes_of(ib_r.at[d, h, 0:15], ib_rs.at[d, h])
            total = ib_r[d, h, 0].astype(F32)
            for z in range(1, CHIPS):
                total = total + ib_r[d, h, z].astype(F32)
            qq[d, h] = total
            squares = squares + jnp.sum(total * total, axis=0, keepdims=True)
        en_s[d:d + 1, :] = squares
        copy_q(d).start()

    def sent(d):
        for h in range(2):
            copy_ia(d, h).wait_send()
            bytes_of(ib_s.at[d, h, 0:15], ib_ss.at[d])
        bytes_of(sa.at[d, 0:15], a_ss.at[d])
        bytes_of(se.at[d, 0:15], e_ss.at[d])
        bytes_of(sh.at[d, 0:15], h_ss.at[d])

    def finish():
        en_r[me] = en_s[...]
        for o in FAR:
            copy_d(o).start()
        bytes_of(en_r.at[0:15], d_rs)
        total = en_r[0]
        for k in range(1, 16):
            total = total + en_r[k]
        et_s[...] = total
        et_r[fq] = total

        def send(o, _):
            step = jnp.where(lax.rem(o, 2) == 1, 16 - o // 2, 16 + o // 2)
            copy_t(lax.rem(fq + step, FREQ)).start()
            return 0

        lax.fori_loop(1, FREQ, send, 0)

        bytes_of(et_r.at[0:31], t_rs)
        total = et_r[0]
        for k in range(1, FREQ):
            total = total + et_r[k]
        copy_q(1).wait_send()
        for d in range(DEPTHS):
            copy_q(d).wait_recv()
            energy = jnp.sum(total[d:d + 1, :], axis=1, keepdims=True)
            scale = lax.rsqrt(energy / (NX * NY) + EPS)
            for h in range(2):
                for rows, got in ((core, qq[d, h]), (1 - core, qp[d, h])):
                    mine = jnp.where(core == 0, got[:, 0:64], got[:, 64:128])
                    img[d, pl.ds(pl.multiple_of(32 * h + 16 * rows, 16), 16), :] = mine * scale

    for h in range(2):
        rows = pl.ds(32 * h, 32)
        pltpu.make_async_copy(spare.at[:, rows], field.at[:, rows], in_sem.at[h]).wait()
        x_radix(32 * h, 32)
        if h == 0:
            more[0].wait()
        if h == 0:
            x_fill(0, FAR, 0, 32)
            x_own(0, 0, 32)
            pl.semaphore_wait(barrier, ROWS + 2)
            x_start(0, FAR, 0, 32)
        else:
            x_out(0, h)
    for d in range(DEPTHS):
        if d == 0:
            relay(wait=False)
            propagator(d)
            relay()
            for c in more[1:]:
                c.wait()
            for b in range(16):
                wb[b, 128:256, 0:128] = -wb[b, 0:128, 128:256]
            relay()
        else:
            relay(signal=False)
            chip_sums(0, 0)
            chip_sums(0, 1)
            propagator(d)
        y_radix(d)
        if d == 0:
            relay()
        y_spectrum()
        if d == 0:
            relay()
        y_back(d)
        if d:
            image_sums(0)
        for h in range(2):
            if d == 0:
                relay()
            x_back(d, h)
            if d and h:
                chip_sums(1, 0)
            correct(d, h)
            if d == 0:
                x_radix(32 * h, 32)
                x_out(1, h)
        if d == 0:
            relay()
    chip_sums(1, 1)
    sent(0)
    sent(1)
    copy_q(0).wait_send()
    image_sums(1)
    finish()

    pltpu.make_async_copy(field, spare, out_sem).wait()

    bytes_of(en_r.at[0:15], d_ss)
    bytes_of(et_r.at[0:31], t_ss)


def shards(wavefield, block_inverse, coefficient, correction_factor, frequencies, slowness):
    tabs = [jnp.asarray(t, BF16) for t in tables()]
    scalars = jnp.concatenate([correction_factor.reshape(2), frequencies, slowness])
    anywhere = pl.BlockSpec(memory_space=pl.ANY)
    hbm = pl.BlockSpec(memory_space=pltpu.HBM)
    vmem = pl.BlockSpec(memory_space=pltpu.VMEM)
    smem = pl.BlockSpec(memory_space=pltpu.SMEM)
    dma = pltpu.SemaphoreType.DMA
    v = pltpu.VMEM
    scratch = [
        v((16, 64, 256), F32),
        v((64, 2048), BF16),
        v((16, 256, 256), BF16),
        v((16, 256, 256), BF16),
        v((4, 4, 128, 256), BF16),
        v((4, 544, 256), BF16),
        v((16, 256, 256), BF16),
        v((16, 64, 256), BF16),
        v((2, 16, 64, 256), BF16),
        v((2, 16, 64, 256), BF16),
        v((4, 256, 256), BF16),
        v((4, 256, 256), F32),
        v((4, 256, 256), BF16),
        v((4, 4, 128, 256), F32),
        v((4, 32, 256), F32),
        v((2, 16, 64, 256), BF16),
        v((2, 16, 64, 256), BF16),
        v((2, 16, 4, 256), F32),
        v((2, 16, 4, 256), F32),
        v((2, 16, 48, 256), F32),
        v((2, 16, 48, 256), F32),
        v((16, 64, 256), F32),
        v((2, 2, 16, 16, 128), BF16),
        v((2, 2, 16, 16, 128), BF16),
        v((2, 2, 16, 16, 128), BF16),
        v((2, 2, 16, 16, 128), BF16),
        v((2, 2, 16, 128), F32),
        v((2, 2, 16, 128), F32),
        v((2, 128), F32),
        v((16, 2, 128), F32),
        v((2, 128), F32),
        v((32, 2, 128), F32),
        dma((2,)), dma((8,)),
        dma((2,)), dma((2, 4)), dma((2,)), dma((2, 2, 4)), dma((2,)), dma((2,)),
        dma((2, 2, 2)), dma((2,)), dma((2, 2)), dma((2, 2)),
        dma, dma, dma, dma, dma,
        pltpu.SemaphoreType.REGULAR, pltpu.SemaphoreType.REGULAR,
    ]
    return pl.pallas_call(
        kernel,
        out_shape=(
            jax.ShapeDtypeStruct((2, 64, 64), F32),
            jax.ShapeDtypeStruct((2, 1, 64, 2048), F32),
        ),
        in_specs=[hbm, hbm, hbm, smem] + [hbm] * 4,
        out_specs=(vmem, anywhere),
        scratch_shapes=scratch,
        compiler_params=pltpu.CompilerParams(
            collective_id=0, has_side_effects=True, vmem_limit_bytes=54525952),
    )(wavefield, block_inverse, coefficient, scalars, *tabs)


def solution(mesh):
    placed = (
        P(None, "freq", "rows", None),
        P(None, "freq", None, None, None),
        P("rows", None),
        P(None, "freq"),
        P("freq"),
        P(),
    )
    return jax.shard_map(
        shards,
        mesh=mesh,
        in_specs=placed,
        out_specs=(P(None, "rows", "freq"), P(None, "freq", "rows", None)),
        check_vma=False,
    )
```

```python
import math

import jax
import jax.numpy as jnp
import numpy as np
from jax import lax
from jax.experimental import pallas as pl
from jax.experimental.pallas import tpu as pltpu
from jax.sharding import PartitionSpec as P

MESH = pl.DeviceIdType.MESH
F32 = jnp.float32
BF16 = jnp.bfloat16
NX = 2048
NY = 1024
DEPTHS = 2
ROWS = 16
FREQ = 32
CHIPS = 16
EPS = 1e-06
EDGES = [64 * j + r for j in range(4) for r in (0, 31, 32, 63)]
FAR = sorted(
    [(dy, dx) for dy in range(4) for dx in range(4) if dy or dx],
    key=lambda o: -(min(o[0], 4 - o[0]) + min(o[1], 4 - o[1])))
SIDES = (2, 1, 3, 0)


def tables():
    b, k2 = np.arange(128)[:, None], np.arange(128)[None, :]
    fwd, inv = [], []
    for k1 in range(16):
        angle = -2.0 * np.pi * ((b * (k1 + 16 * k2)) % NX) / NX
        re, im = np.cos(angle), np.sin(angle)
        block = np.block([[re, im], [-im, re]])
        fwd.append(block)
        inv.append(block.T / NX)
    k2, b = np.arange(256)[:, None], np.arange(256)[None, :]
    yfwd, yinv = [], []
    for k1 in range(4):
        angle = -2.0 * np.pi * ((b * (k1 + 4 * k2)) % NY) / NY
        re, im = np.cos(angle), np.sin(angle)
        yfwd.append([np.concatenate([re[64 * m:64 * m + 64], im[64 * m:64 * m + 64]], 0) for m in range(4)])
        re, im = re.T / NY, -im.T / NY
        rows = [part[64 * j:64 * j + 64] for j in range(4) for part in (re, im)]
        yinv.append(np.concatenate(rows + [re[EDGES], im[EDGES]], 0))
    return [np.stack(t).astype(np.float32) for t in (fwd, inv, yfwd, yinv)]


def add(p, q):
    return p[0] + q[0], p[1] + q[1]


def sub(p, q):
    return p[0] - q[0], p[1] - q[1]


def fft4(x, sign):
    a, b = add(x[0], x[2]), sub(x[0], x[2])
    c, d = add(x[1], x[3]), sub(x[1], x[3])
    turned = (-sign * d[1], sign * d[0]) if sign > 0 else (d[1], -d[0])
    return [add(a, c), add(b, turned), sub(a, c), sub(b, turned)]


def twist(p, m, sign):
    re, im = p
    if m == 0:
        return p
    if m == 4:
        return (-im, re) if sign > 0 else (im, -re)
    if m == 2:
        h = math.sqrt(0.5)
        return ((re - im) * h, (re + im) * h) if sign > 0 else ((re + im) * h, (im - re) * h)
    c, s = math.cos(2 * math.pi * m / 16), sign * math.sin(2 * math.pi * m / 16)
    return re * c - im * s, re * s + im * c


def fft16(x, sign):
    inner = [fft4([x[4 * n1 + n2] for n1 in range(4)], sign) for n2 in range(4)]
    out = [None] * 16
    for k1 in range(4):
        got = fft4([twist(inner[n2][k1], n2 * k1, sign) for n2 in range(4)], sign)
        for k2 in range(4):
            out[k1 + 4 * k2] = got[k2]
    return out


def sin_cos(r):
    n = jnp.floor(r * (2.0 / math.pi) + 0.5)
    t = (r - n * 1.5703125) - n * (math.pi / 2 - 1.5703125)
    t2 = t * t
    sine = t + t * t2 * (-1 / 6 + t2 * (1 / 120 + t2 * (-1 / 5040 + t2 * (1 / 362880))))
    cosine = 1.0 + t2 * (-0.5 + t2 * (1 / 24 + t2 * (-1 / 720 + t2 * (1 / 40320))))
    m = n - 4.0 * jnp.floor(n * 0.25)
    odd = (m == 1.0) | (m == 3.0)
    s, c = jnp.where(odd, cosine, sine), jnp.where(odd, sine, cosine)
    return jnp.where(m >= 2.0, -s, s), jnp.where((m == 1.0) | (m == 2.0), -c, c)


def kernel(
    wf, bi, coef_h, scalars, tx_h, txi_h, ty_h, tyi_h,
    img, fin,
    field, coef, tx, txi, ty, tyi, wb, xb, sa, ra, yb, uu, cb, gg, gh, se, re_, sh, rh, gx, sp, spare,
    ia_s, ia_r, ib_s, ib_r, qq, qp, en_s, en_r, et_s, et_r,
    in_sem, tab_sem, a_ss, a_rs, e_ss, e_rs, h_ss, h_rs, ia_sem, ib_ss, ib_rs, q_sem,
    d_ss, d_rs, t_ss, t_rs, out_sem, up_sem, down_sem,
):
    me = lax.axis_index("rows")
    fq = lax.axis_index("freq")
    my_y, my_x = me // 4, lax.rem(me, 4)
    chip, core = fq // 2, lax.rem(fq, 2)
    partner = chip * 2 + (1 - core)

    barrier = pltpu.get_barrier_semaphore()

    def greet_rows(o, _):
        pl.semaphore_signal(barrier, inc=1, device_id={"rows": lax.rem(me + o, ROWS)}, device_id_type=MESH)
        return 0

    lax.fori_loop(1, ROWS, greet_rows, 0)
    above = lax.rem(chip + 1, CHIPS) * 2 + core
    below = lax.rem(chip + CHIPS - 1, CHIPS) * 2 + core
    for to in (partner, above, below):
        pl.semaphore_signal(barrier, inc=1, device_id={"freq": to}, device_id_type=MESH)

    def relay(wait=True, signal=True):
        if wait:
            pl.semaphore_wait(up_sem, 1)
            pl.semaphore_wait(down_sem, 1)
        if signal:
            pl.semaphore_signal(up_sem, inc=1, device_id={"freq": above}, device_id_type=MESH)
            pl.semaphore_signal(down_sem, inc=1, device_id={"freq": below}, device_id_type=MESH)

    loads = []
    for h in range(2):
        rows = pl.ds(32 * h, 32)
        for part in range(2):
            for a in range(16):
                loads.append(pltpu.make_async_copy(
                    wf.at[part, 0, rows, pl.ds(128 * a, 128)],
                    field.at[a, rows, pl.ds(128 * part, 128)], in_sem.at[h]))
    more = [pltpu.make_async_copy(s, d, tab_sem.at[i]) for i, (s, d) in enumerate((
        (tx_h, tx), (ty_h, ty), (tyi_h, tyi), (txi_h, txi), (coef_h, coef),
        (bi.at[0, 0], wb.at[:, pl.ds(0, 128), pl.ds(0, 128)]),
        (bi.at[0, 0], wb.at[:, pl.ds(128, 128), pl.ds(128, 128)]),
        (bi.at[1, 0], wb.at[:, pl.ds(0, 128), pl.ds(128, 128)]),
    ))]
    for c in loads[:32] + more[:1] + loads[32:] + more[1:]:
        c.start()

    def peer(o):
        return lax.rem(my_y + o[0], 4) * 4 + lax.rem(my_x + o[1], 4)

    def source(o):
        return peer((4 - o[0], 4 - o[1]))

    def copy_a(d, o, first, count):
        rows = pl.ds(first, count)
        return pltpu.make_async_remote_copy(
            sa.at[d, peer(o), rows], ra.at[d, me, rows], a_ss.at[d], a_rs.at[d, o[1]],
            device_id={"rows": peer(o)}, device_id_type=MESH)

    def copy_e(d, o, h):
        rows = pl.ds(32 * h, 32)
        return pltpu.make_async_remote_copy(
            se.at[d, peer(o), rows], re_.at[d, me, rows], e_ss.at[d], e_rs.at[d, h, o[1]],
            device_id={"rows": peer(o)}, device_id_type=MESH)

    def copy_h(d, o):
        return pltpu.make_async_remote_copy(
            sh.at[d, peer(o)], rh.at[d, me], h_ss.at[d], h_rs.at[d],
            device_id={"rows": peer(o)}, device_id_type=MESH)

    def copy_ia(d, h):
        return pltpu.make_async_remote_copy(
            ia_s.at[d, h], ia_r.at[d, h], ia_sem.at[0, d, h], ia_sem.at[1, d, h],
            device_id={"freq": partner}, device_id_type=MESH)

    def copy_ib(d, h, to):
        return pltpu.make_async_remote_copy(
            ib_s.at[d, h, to], ib_r.at[d, h, chip], ib_ss.at[d], ib_rs.at[d, h],
            device_id={"freq": to * 2 + core}, device_id_type=MESH)

    def copy_q(d):
        return pltpu.make_async_remote_copy(
            qq.at[d], qp.at[d], q_sem.at[0, d], q_sem.at[1, d],
            device_id={"freq": partner}, device_id_type=MESH)

    def copy_d(o):
        return pltpu.make_async_remote_copy(
            en_s, en_r.at[me], d_ss, d_rs,
            device_id={"rows": peer(o)}, device_id_type=MESH)

    def copy_t(to):
        return pltpu.make_async_remote_copy(
            et_s, et_r.at[fq], t_ss, t_rs,
            device_id={"freq": to}, device_id_type=MESH)

    def bytes_of(ref, sem):
        pltpu.make_async_copy(ref, ref, sem).wait()

    def x_radix(first, count):
        def rows(c, _):
            r = pl.ds(pl.multiple_of(c * 16, 16), 16)
            ys = fft16([(field[a, r, 0:128], field[a, r, 128:256]) for a in range(16)], -1)
            for k in range(16):
                xb[k, r, 0:128] = ys[k][0].astype(BF16)
                xb[k, r, 128:256] = ys[k][1].astype(BF16)
            return 0

        lax.fori_loop(first // 16, (first + count) // 16, rows, 0)

    def x_block(k, rows):
        return jnp.dot(xb[k, rows], tx[k], preferred_element_type=F32).astype(BF16)

    def x_fill(d, some, first, count):
        rows = slice(first, first + count)
        for o in some:
            sa[d, peer(o), rows] = x_block(peer(o), rows)

    def x_own(d, first, count):
        rows = slice(first, first + count)
        ra[d, me, rows] = x_block(me, rows)

    def x_start(d, some, first, count):
        for o in some:
            copy_a(d, o, first, count).start()

    def propagator(d):
        omega = scalars[2] * scalars[3 + d]
        omega2 = omega * omega

        def rows(c, _):
            k1, base = c // 16, lax.rem(c, 16) * 16
            ky = k1 + 4 * (base + lax.broadcasted_iota(jnp.int32, (16, 128), 0))
            kx = me + 16 * lax.broadcasted_iota(jnp.int32, (16, 128), 1)
            ky = jnp.where(2 * ky < NY, ky, ky - NY).astype(F32) * (2.0 * math.pi / NY)
            kx = jnp.where(2 * kx < NX, kx, kx - NX).astype(F32) * (2.0 * math.pi / NX)
            q = omega2 - ky * ky - kx * kx
            root = jnp.sqrt(jnp.abs(q))
            s, co = sin_cos(root)
            up = q >= 0.0
            r = pl.ds(pl.multiple_of(base, 16), 16)
            uu[k1, r, 0:128] = jnp.where(up, co, jnp.exp(-root))
            uu[k1, r, 128:256] = jnp.where(up, s, 0.0)
            return 0

        lax.fori_loop(0, 64, rows, 0)

    def y_radix(d):
        for dx in SIDES:
            j = lax.rem(my_x + 4 - dx, 4)
            bytes_of(ra.at[d, 0:4 if dx else 3], a_rs.at[d, dx])

            def rows(c, _):
                r = pl.ds(pl.multiple_of(c * 16, 16), 16)
                ys = fft4([
                    (ra[d, 4 * a + j, r, 0:128].astype(F32), ra[d, 4 * a + j, r, 128:256].astype(F32))
                    for a in range(4)], -1)
                o = pl.ds(pl.multiple_of(j * 64 + c * 16, 16), 16)
                for k in range(4):
                    yb[k, o, 0:128] = ys[k][0].astype(BF16)
                    yb[k, o, 128:256] = ys[k][1].astype(BF16)
                return 0

            lax.fori_loop(0, 4, rows, 0)

    def y_spectrum():
        for k in range(4):
            for m in range(4):
                got = jnp.dot(ty[k, m], yb[k], preferred_element_type=F32)
                top, low = got[0:64], got[64:128]
                br = top[:, 0:128] - low[:, 128:256]
                bm = top[:, 128:256] + low[:, 0:128]
                r = slice(64 * m, 64 * m + 64)
                ur, um = uu[k, r, 0:128], uu[k, r, 128:256]
                cb[k, r, 0:128] = (br * ur - bm * um).astype(BF16)
                cb[k, r, 128:256] = (br * um + bm * ur).astype(BF16)

    def y_back(d):
        for k in range(4):
            gh[k] = jnp.dot(tyi[k, 512:544], cb[k], preferred_element_type=F32)
        edge = fft4([
            (gh[k, 0:16, 0:128] - gh[k, 16:32, 128:256], gh[k, 0:16, 128:256] + gh[k, 16:32, 0:128])
            for k in range(4)], 1)
        zero = jnp.zeros((1, 128), F32)
        for s in range(16):
            for p in range(2):
                lanes = slice(128 * p, 128 * p + 128)
                for row, (t, e) in enumerate(((s - 1, 3), (s, 2), (s, 1), (s + 1, 0))):
                    at = 4 * (t % 4) + e
                    sh[d, s, row:row + 1, lanes] = edge[t // 4][p][at:at + 1] if 0 <= t < 16 else zero
        rh[d, me] = sh[d, me]
        for o in FAR:
            copy_h(d, o).start()
        def lines(dx):
            j = lax.rem(my_x + dx, 4)
            for k in range(4):
                gg[dx, k] = jnp.dot(
                    tyi[k, pl.ds(pl.multiple_of(128 * j, 128), 128)], cb[k], preferred_element_type=F32)

        lines(SIDES[0])
        for turn, dx in enumerate(SIDES):
            j = lax.rem(my_x + dx, 4)
            if turn < 3:
                lines(SIDES[turn + 1])
            for c in range(4):
                r, r2 = slice(16 * c, 16 * c + 16), slice(64 + 16 * c, 80 + 16 * c)
                es = fft4([
                    (gg[dx, k, r, 0:128] - gg[dx, k, r2, 128:256], gg[dx, k, r, 128:256] + gg[dx, k, r2, 0:128])
                    for k in range(4)], 1)
                for a in range(4):
                    for p in range(2):
                        se[d, 4 * a + j, r, 128 * p:128 * p + 128] = es[a][p].astype(BF16)
            for dy in (2, 1, 3, 0):
                if dx or dy:
                    copy_e(d, (dy, dx), 0).start()
        re_[d, me] = se[d, me]
        for o in FAR:
            copy_e(d, o, 1).start()

    def x_back(d, h):
        if h == 0:
            bytes_of(rh.at[d, 0:15], h_rs.at[d])
        for o in [(dy, dx) for dx in SIDES for dy in (2, 1, 3, 0)]:
            k = source(o)
            if o[0] == 2:
                bytes_of(re_.at[d, 0:4 if o[1] else 3, 0:32], e_rs.at[d, h, o[1]])
            halo = jnp.concatenate([rh[d, k, 2 * h:2 * h + 2], jnp.zeros((14, 256), F32)], 0)
            rows = jnp.concatenate([re_[d, k, 32 * h:32 * h + 32], halo.astype(BF16)], 0)
            gx[h, k] = jnp.dot(rows, txi[k], preferred_element_type=F32)

        def rows(c, _):
            r = pl.ds(pl.multiple_of(c * 16, 16), 16)
            ss = fft16([(gx[h, k, r, 0:128], gx[h, k, r, 128:256]) for k in range(16)], 1)
            o = pl.ds(pl.multiple_of(8 + c * 16, 8), 16)
            for a in range(16):
                sp[h, a, o, 0:128] = ss[a][0]
                sp[h, a, o, 128:256] = ss[a][1]
            return 0

        lax.fori_loop(0, 2, rows, 0)
        ss = fft16([(gx[h, k, 32:40, 0:128], gx[h, k, 32:40, 128:256]) for k in range(16)], 1)
        for a in range(16):
            for p in range(2):
                sp[h, a, 7:8, 128 * p:128 * p + 128] = ss[a][p][0:1]
                sp[h, a, 40:41, 128 * p:128 * p + 128] = ss[a][p][1:2]

    def correct(d, h):
        gr, gi = scalars[0], scalars[1]
        own = slice(32 * h, 32 * h + 32)
        for b in range(16):
            around = sp[h, b]
            s0 = around[8:40]
            lo = pltpu.roll(around, 1, 0)[8:40]
            hi = pltpu.roll(around, 47, 0)[8:40]
            curve = hi - 2.0 * s0 + lo
            cl, ci = curve[:, 0:128], curve[:, 128:256]
            co = coef[own, 128 * b:128 * b + 128].astype(F32)
            cr, cm = co * gr, co * gi
            rr = s0[:, 0:128] + (cr * cl - cm * ci)
            ri = s0[:, 128:256] + (cr * ci + cm * cl)
            r = jnp.concatenate([rr, ri], 1)
            field[b, own] = r + jnp.dot(r.astype(BF16), wb[b], preferred_element_type=F32)
        half = pl.ds(pl.multiple_of(32 * h + 16 * (1 - core), 16), 16)
        for b in range(16):
            ia_s[d, h, b] = field[b, half, 0:128].astype(BF16)
        copy_ia(d, h).start()
        if d == DEPTHS - 1:
            for b in range(16):
                for part in range(2):
                    store(b, part, h).start()

    def store(b, part, h):
        return pltpu.make_async_copy(
            field.at[b, pl.ds(32 * h, 32), pl.ds(128 * part, 128)],
            fin.at[part, 0, pl.ds(32 * h, 32), pl.ds(128 * b, 128)], out_sem)

    def chip_sums(d, h):
        copy_ia(d, h).wait_recv()
        half = pl.ds(pl.multiple_of(32 * h + 16 * core, 16), 16)
        for b in range(16):
            ib_s[d, h, b] = (field[b, half, 0:128] + ia_r[d, h, b].astype(F32)).astype(BF16)
        ib_r[d, h, chip] = ib_s[d, h, chip]

        def send(o, _):
            step = jnp.where(lax.rem(o, 2) == 1, 8 - o // 2, 8 + o // 2)
            copy_ib(d, h, lax.rem(chip + step, CHIPS)).start()
            return 0

        lax.fori_loop(1, CHIPS, send, 0)

    def image_sums(d):
        squares = jnp.zeros((1, 128), F32)
        for h in range(2):
            bytes_of(ib_r.at[d, h, 0:15], ib_rs.at[d, h])
            total = ib_r[d, h, 0].astype(F32)
            for z in range(1, CHIPS):
                total = total + ib_r[d, h, z].astype(F32)
            qq[d, h] = total
            squares = squares + jnp.sum(total * total, axis=0, keepdims=True)
        en_s[d:d + 1, :] = squares
        copy_q(d).start()

    def sent(d):
        for h in range(2):
            copy_ia(d, h).wait_send()
            bytes_of(ib_s.at[d, h, 0:15], ib_ss.at[d])
        bytes_of(sa.at[d, 0:15], a_ss.at[d])
        bytes_of(se.at[d, 0:15], e_ss.at[d])
        bytes_of(sh.at[d, 0:15], h_ss.at[d])

    def finish():
        en_r[me] = en_s[...]
        for o in FAR:
            copy_d(o).start()
        bytes_of(en_r.at[0:15], d_rs)
        total = en_r[0]
        for k in range(1, 16):
            total = total + en_r[k]
        et_s[...] = total
        et_r[fq] = total

        def send(o, _):
            step = jnp.where(lax.rem(o, 2) == 1, 16 - o // 2, 16 + o // 2)
            copy_t(lax.rem(fq + step, FREQ)).start()
            return 0

        lax.fori_loop(1, FREQ, send, 0)

        bytes_of(et_r.at[0:31], t_rs)
        total = et_r[0]
        for k in range(1, FREQ):
            total = total + et_r[k]
        copy_q(1).wait_send()
        for d in range(DEPTHS):
            copy_q(d).wait_recv()
            energy = jnp.sum(total[d:d + 1, :], axis=1, keepdims=True)
            scale = lax.rsqrt(energy / (NX * NY) + EPS)
            for h in range(2):
                for rows, got in ((core, qq[d, h]), (1 - core, qp[d, h])):
                    mine = jnp.where(core == 0, got[:, 0:64], got[:, 64:128])
                    img[d, pl.ds(pl.multiple_of(32 * h + 16 * rows, 16), 16), :] = mine * scale

    for h in range(2):
        rows = pl.ds(32 * h, 32)
        pltpu.make_async_copy(spare.at[:, rows], field.at[:, rows], in_sem.at[h]).wait()
        x_radix(32 * h, 32)
        if h == 0:
            more[0].wait()
        x_fill(0, FAR, 32 * h, 32)
        x_own(0, 32 * h, 32)
        if h == 0:
            pl.semaphore_wait(barrier, ROWS + 2)
        x_start(0, FAR, 32 * h, 32)
    for d in range(DEPTHS):
        if d == 0:
            relay(wait=False)
            propagator(d)
            relay()
            for c in more[1:]:
                c.wait()
            for b in range(16):
                wb[b, 128:256, 0:128] = -wb[b, 0:128, 128:256]
            relay()
        else:
            relay(signal=False)
            chip_sums(0, 0)
            chip_sums(0, 1)
            propagator(d)
        y_radix(d)
        if d == 0:
            relay()
        y_spectrum()
        if d == 0:
            relay()
        y_back(d)
        if d:
            image_sums(0)
        for h in range(2):
            if d == 0:
                relay()
            x_back(d, h)
            if d and h:
                chip_sums(1, 0)
            correct(d, h)
            if d == 0:
                x_radix(32 * h, 32)
                x_fill(1, FAR, 32 * h, 32)
                x_own(1, 32 * h, 32)
                x_start(1, FAR, 32 * h, 32)
        if d == 0:
            relay()
    chip_sums(1, 1)
    sent(0)
    sent(1)
    copy_q(0).wait_send()
    image_sums(1)
    finish()

    pltpu.make_async_copy(field, spare, out_sem).wait()

    bytes_of(en_r.at[0:15], d_ss)
    bytes_of(et_r.at[0:31], t_ss)


def shards(wavefield, block_inverse, coefficient, correction_factor, frequencies, slowness):
    tabs = [jnp.asarray(t, BF16) for t in tables()]
    scalars = jnp.concatenate([correction_factor.reshape(2), frequencies, slowness])
    anywhere = pl.BlockSpec(memory_space=pl.ANY)
    hbm = pl.BlockSpec(memory_space=pltpu.HBM)
    vmem = pl.BlockSpec(memory_space=pltpu.VMEM)
    smem = pl.BlockSpec(memory_space=pltpu.SMEM)
    dma = pltpu.SemaphoreType.DMA
    v = pltpu.VMEM
    scratch = [
        v((16, 64, 256), F32),
        v((64, 2048), BF16),
        v((16, 256, 256), BF16),
        v((16, 256, 256), BF16),
        v((4, 4, 128, 256), BF16),
        v((4, 544, 256), BF16),
        v((16, 256, 256), BF16),
        v((16, 64, 256), BF16),
        v((2, 16, 64, 256), BF16),
        v((2, 16, 64, 256), BF16),
        v((4, 256, 256), BF16),
        v((4, 256, 256), F32),
        v((4, 256, 256), BF16),
        v((4, 4, 128, 256), F32),
        v((4, 32, 256), F32),
        v((2, 16, 64, 256), BF16),
        v((2, 16, 64, 256), BF16),
        v((2, 16, 4, 256), F32),
        v((2, 16, 4, 256), F32),
        v((2, 16, 48, 256), F32),
        v((2, 16, 48, 256), F32),
        v((16, 64, 256), F32),
        v((2, 2, 16, 16, 128), BF16),
        v((2, 2, 16, 16, 128), BF16),
        v((2, 2, 16, 16, 128), BF16),
        v((2, 2, 16, 16, 128), BF16),
        v((2, 2, 16, 128), F32),
        v((2, 2, 16, 128), F32),
        v((2, 128), F32),
        v((16, 2, 128), F32),
        v((2, 128), F32),
        v((32, 2, 128), F32),
        dma((2,)), dma((8,)),
        dma((2,)), dma((2, 4)), dma((2,)), dma((2, 2, 4)), dma((2,)), dma((2,)),
        dma((2, 2, 2)), dma((2,)), dma((2, 2)), dma((2, 2)),
        dma, dma, dma, dma, dma,
        pltpu.SemaphoreType.REGULAR, pltpu.SemaphoreType.REGULAR,
    ]
    return pl.pallas_call(
        kernel,
        out_shape=(
            jax.ShapeDtypeStruct((2, 64, 64), F32),
            jax.ShapeDtypeStruct((2, 1, 64, 2048), F32),
        ),
        in_specs=[hbm, hbm, hbm, smem] + [hbm] * 4,
        out_specs=(vmem, anywhere),
        scratch_shapes=scratch,
        compiler_params=pltpu.CompilerParams(
            collective_id=0, has_side_effects=True, vmem_limit_bytes=54525952),
    )(wavefield, block_inverse, coefficient, scalars, *tabs)


def solution(mesh):
    placed = (
        P(None, "freq", "rows", None),
        P(None, "freq", None, None, None),
        P("rows", None),
        P(None, "freq"),
        P("freq"),
        P(),
    )
    return jax.shard_map(
        shards,
        mesh=mesh,
        in_specs=placed,
        out_specs=(P(None, "rows", "freq"), P(None, "freq", "rows", None)),
        check_vma=False,
    )
```
